512 devices in a mesh: context: 32 (over y, x), tensor: 16 (over z, core).
Axes of the slice: x: 4, y: 8, z: 8, core: 2. Of those that a mesh axis runs over, the one named last changes fastest.
Arguments:
- queries: bfloat16 [1, 16384, 4096], P(None, 'context', 'tensor'), may hold values from -6 to 6
- keys: bfloat16 [1, 16384, 4096], P(None, 'context', 'tensor'), may hold values from -0.546875 to 0.546875
- spike_counts: int32 [1, 16384, 4096], P(None, 'context', 'tensor'), may hold values from -4 to 4
- spike_scale: float32 [4096], P('tensor'), may hold values from 0.5 to 2
- log_decay: float32 [1, 32, 16384], P(None, 'tensor', 'context'), may hold values from -3 to 0, as said below
- norm_gain: float32 [4096], P('tensor'), may hold values from 0.5 to 1.5
- out_weight: bfloat16 [4096, 8192], P('context', 'tensor'), may hold values from -0.09375 to 0.09375
- residual_in: bfloat16 [1, 16384, 8192], P(None, 'context', 'tensor'), may hold values from -6 to 6
Outputs:
- residual_out: bfloat16 [1, 16384, 8192], P(None, 'context', 'tensor')
The draws below stay inside these ranges and needn't reach their ends.
Inputs may be any that keep to these rules, and one draw needn't show every extreme that they name: log_decay is negative.
All inputs are finite; a program needn't handle non-finite values.
Results may differ from the reference program's by a relative error of at most 0.0095.
Values may be sent and summed in bfloat16 or wider, within the bound.
A program may use at most 64 MiB of HBM per device.

```python
import math
import jax
import jax.numpy as jnp
from jax import lax

D = 8192
HS = 128
HEADS = 32
GROUP = 512
NUM_QUERIES_IN = 1
TEXT_SPAN = 16384
N_CONTEXT = 32


def draw_log_decay(key, part):
    entire_lookup_matrix = jax.random.split(jax.random.fold_in(key, 17), 7)
    fast = jax.random.randint(entire_lookup_matrix[0], (NUM_QUERIES_IN, HEADS, 1), 0, 2) == 0
    fast_rate = 2.3 / min(40, GROUP // 4) * jnp.exp(jax.random.uniform(entire_lookup_matrix[1], (NUM_QUERIES_IN, HEADS, 1), jnp.float32, 0.0, 0.69))
    slow_rate = 2.3 / TEXT_SPAN * jax.random.uniform(entire_lookup_matrix[2], (NUM_QUERIES_IN, HEADS, 1), jnp.float32, 0.03, 0.2)
    opening_ordinal = jnp.where(fast, fast_rate, slow_rate)
    piece_dampening_multiplier = jnp.exp(jax.random.uniform(entire_lookup_matrix[3], (NUM_QUERIES_IN, HEADS, TEXT_SPAN // GROUP), jnp.float32, 0.0, 0.92))
    piece_dampening_multiplier = jnp.repeat(piece_dampening_multiplier, GROUP, axis=2)
    lexeme_dampening_multiplier = jax.random.uniform(entire_lookup_matrix[4], (NUM_QUERIES_IN, HEADS, TEXT_SPAN), jnp.float32, 0.5, 1.5)
    piece_ordinal = jax.random.randint(entire_lookup_matrix[5], (NUM_QUERIES_IN, 1, 2), 0, TEXT_SPAN)
    piece_attenuation_total = jax.random.uniform(entire_lookup_matrix[6], (NUM_QUERIES_IN, 1, 2), jnp.float32, 0.2, 0.45)
    vocabulary_identifiers = jnp.arange(TEXT_SPAN)[None, None, :, None]
    active_pieces = jnp.sum(jnp.where(vocabulary_identifiers == piece_ordinal[:, :, None, :], jnp.log(1.0 - piece_attenuation_total)[:, :, None, :], 0.0), axis=3)
    combined = -(opening_ordinal * piece_dampening_multiplier * lexeme_dampening_multiplier) + active_pieces
    return jnp.maximum(combined, -3.0).astype(jnp.float32)


def set_ends(result, own_key, smallest, high):
    index_at = [jax.random.randint(jax.random.fold_in(own_key, axis), (), 0, length) for axis, length in enumerate(result.shape)]
    widest = result.shape.index(max(result.shape))
    next_to = index_at[:widest] + [(index_at[widest] + 1) % result.shape[widest]] + index_at[widest + 1:]
    return result.at[tuple(index_at)].set(smallest).at[tuple(next_to)].set(high)


def levels(key, shape, cuts, low, top_value):
    gain = 1.0
    for dim, shards_of in cuts:
        steps = jax.random.uniform(jax.random.fold_in(jax.random.fold_in(key, 6), dim), (shards_of,), jnp.float32, low / len(cuts), top_value / len(cuts))
        gain = gain * jnp.repeat(jnp.exp(steps), shape[dim] // shards_of).reshape((-1,) + (1,) * (len(shape) - 1 - dim))
    return gain


def gaussian(rng, shape, spread, bound, pieces=(), kind=jnp.bfloat16):
    values = jax.random.normal(rng, shape, jnp.float32) * spread
    if len(pieces) > 0:
        values = levels(rng, shape, pieces, -0.22, 0.18) * values
    return jnp.clip(values, min=-bound, max=bound).astype(kind)


def setup_inputs(seed: int = 0) -> dict:
    key_list = jax.random.split(jax.random.key(seed), 9)
    queries = gaussian(key_list[0], (NUM_QUERIES_IN, TEXT_SPAN, HEADS * HS), 1.0, 6.0, ((1, 32), (2, 16)))
    keys = gaussian(key_list[1], (NUM_QUERIES_IN, TEXT_SPAN, HEADS * HS), 0.088, 0.546875, ((1, 32), (2, 16)))
    spike_counts = set_ends(jax.random.randint(key_list[2], (NUM_QUERIES_IN, TEXT_SPAN, HEADS * HS), -4, 5), jax.random.fold_in(key_list[2], 1), -4, 4).astype(jnp.int32)
    spike_scale = jnp.clip(jnp.exp(math.log(2.0) - 1.3862944 * jax.random.uniform(key_list[3], (HEADS * HS,), jnp.float32) ** levels(key_list[3], (HEADS * HS,), ((0, 16),), -0.2, 0.2)), 0.5, 2.0)
    log_decay = draw_log_decay(jax.random.fold_in(key_list[8], 71), 0)
    norm_gain = jnp.clip(1.0 + 0.1 * jax.random.normal(key_list[5], (HEADS * HS,), jnp.float32), 0.5, 1.5)
    out_weight = gaussian(key_list[6], (HEADS * HS, D), (HEADS * HS) ** -0.5, 0.09375, ((0, 32), (1, 16)))
    residual_in = gaussian(key_list[7], (NUM_QUERIES_IN, TEXT_SPAN, D), 1.0, 6.0, ((1, 32), (2, 16)))
    return {"queries": queries, "keys": keys, "spike_counts": spike_counts, "spike_scale": spike_scale, "log_decay": log_decay, "norm_gain": norm_gain, "out_weight": out_weight, "residual_in": residual_in}


epsilon = 1e-06

def rounded(array):
    return lax.optimization_barrier(array.astype(jnp.bfloat16)).astype(jnp.float32)

def one_request(queries, keys, values, log_decay, norm_gain):
    heads = log_decay.shape[0]
    head_size = queries.shape[1] // heads
    block = TEXT_SPAN // N_CONTEXT
    highest = lax.Precision.HIGHEST

    def split_heads(array, start):
        piece = lax.dynamic_slice_in_dim(array, start, block, 0)
        return piece.reshape(block, heads, head_size).transpose(1, 0, 2).astype(jnp.float32)

    def advance(state, index):
        start = (index * block).astype(jnp.int32)
        query_blk = split_heads(queries, start)
        key_blk = split_heads(keys, start)
        value_blk = split_heads(values, start)
        rates = lax.dynamic_slice_in_dim(log_decay, start, block, 1)
        cumulative = jnp.cumsum(rates, axis=1)
        vocabulary_identifiers = jnp.arange(block)
        causal = vocabulary_identifiers[:, None] >= vocabulary_identifiers[None, :]
        gaps = cumulative[:, :, None] - cumulative[:, None, :]
        decay_mat = jnp.exp(jnp.where(causal[None], gaps, -1e+30))
        scores = jnp.einsum('htd,hsd->hts', query_blk, key_blk, precision=highest)
        weights = rounded(scores * decay_mat)
        intra = jnp.einsum('hts,hsd->htd', weights, value_blk, precision=highest)
        carried = jnp.exp(cumulative)[:, :, None] * jnp.einsum('htd,hde->hte', query_blk, state, precision=highest)
        mixed = intra + carried
        to_end = jnp.exp(cumulative[:, -1:] - cumulative)
        weighted_keys = rounded(key_blk * to_end[:, :, None])
        own_state = jnp.einsum('hsd,hse->hde', weighted_keys, value_blk, precision=highest)
        new_state = jnp.exp(cumulative[:, -1])[:, None, None] * state + own_state
        scale = lax.rsqrt(lax.optimization_barrier(jnp.mean(mixed * mixed, axis=-1, keepdims=True)) + epsilon)
        normed = (mixed * scale * norm_gain.reshape(heads, 1, head_size)).astype(jnp.bfloat16)
        return (new_state, normed.transpose(1, 0, 2).reshape(block, heads * head_size))
    start_state = jnp.zeros((heads, head_size, head_size), jnp.float32)
    _, blocks = lax.scan(advance, start_state, jnp.arange(N_CONTEXT, dtype=jnp.int32))
    return blocks.reshape(TEXT_SPAN, heads * head_size)

def reference(queries, keys, spike_counts, spike_scale, log_decay, norm_gain, out_weight, residual_in):
    values = (spike_counts.astype(jnp.float32) * spike_scale).astype(jnp.bfloat16)
    outputs = []
    for request in range(NUM_QUERIES_IN):
        normed = one_request(queries[request], keys[request], values[request], log_decay[request], norm_gain)
        projected = jnp.dot(normed, out_weight, preferred_element_type=jnp.float32)
        outputs.append((residual_in[request].astype(jnp.float32) + projected).astype(jnp.bfloat16))
    return jnp.stack(outputs)
```

```python
import functools

import jax
import jax.numpy as jnp
from jax import lax
from jax.experimental import pallas as pl
from jax.experimental.pallas import tpu as pltpu
from jax.sharding import PartitionSpec as P

MESH = pl.DeviceIdType.MESH
NX = 4
EPSILON = 1e-06
F32 = jnp.float32
BF16 = jnp.bfloat16
NT = (((1,), (1,)), ((), ()))
TN = (((0,), (0,)), ((), ()))


class Net:
    def __init__(self, send_sem, recv_sem):
        self.send_sem, self.recv_sem = send_sem, recv_sem
        self.number = {}
        self.sent = []

    def slot(self, name):
        return self.number.setdefault(name, len(self.number))

    def copy(self, name, src, dst, target):
        i = self.slot(name)
        return pltpu.make_async_remote_copy(
            src_ref=src,
            dst_ref=dst,
            send_sem=self.send_sem.at[i],
            recv_sem=self.recv_sem.at[i],
            device_id=target,
            device_id_type=MESH,
        )

    def send(self, name, src, dst, target, when=None):
        copy = self.copy(name, src, dst, target)
        if when is None:
            copy.start()
        else:
            pl.when(when)(copy.start)
        self.sent.append((copy, when))

    def arrive(self, name, place, source, when=None):
        copy = self.copy(name, place, place, source)
        if when is None:
            copy.wait_recv()
        else:
            pl.when(when)(copy.wait_recv)

    def drain(self):
        for copy, when in self.sent:
            if when is None:
                copy.wait_send()
            else:
                pl.when(when)(copy.wait_send)


def kernel(
    dims,
    q_hbm, k_hbm, cnt_hbm, scale_ref, ld_ref, gain_ref, w_hbm, res_hbm, out_hbm,
    q, k, cnt, res, v, acc, out, tri, col, intra, a_all, w_all,
    p1_send, p1_recv, p2_send, p2_recv, p3_send, p3_recv,
    send_sem, recv_sem, load_sem,
):
    ny, nz, heads, hs, block, wrows, xr = dims
    ctx, ten = lax.axis_index("context"), lax.axis_index("tensor")
    y, x = ctx // NX, ctx % NX
    z, core = ten // 2, ten % 2
    quarter = hs // NX
    half = block // 2
    ry, rz = ny // 2, nz // 2
    yr = wrows - xr

    def yp(d):
        return lax.rem(y + (d + ny), ny)

    def xp(d):
        return lax.rem(x + (d + NX), NX)

    def zp(d):
        return lax.rem(z + (d + nz), nz)

    def at_y(d):
        return (yp(d) * NX + x, ten)

    def at_x(d):
        return (y * NX + xp(d), ten)

    def at_z(d):
        return (ctx, zp(d) * 2 + core)

    partner = (ctx, z * 2 + (1 - core))
    net = Net(send_sem, recv_sem)

    loads = [
        pltpu.make_async_copy(k_hbm.at[0], k, load_sem.at[0]),
        pltpu.make_async_copy(cnt_hbm.at[0], cnt, load_sem.at[1]),
        pltpu.make_async_copy(w_hbm, w_all.at[ctx], load_sem.at[2]),
        pltpu.make_async_copy(q_hbm.at[0], q, load_sem.at[3]),
        pltpu.make_async_copy(res_hbm.at[0], res, load_sem.at[4]),
    ]
    for load in loads:
        load.start()
    barrier = pltpu.get_barrier_semaphore()
    friends = [at_y(d) for d in range(1, ny)] + [at_x(d) for d in range(1, NX)]
    friends += [at_z(1), at_z(-1), partner]
    for friend in friends:
        pl.semaphore_signal(barrier, inc=1, device_id=friend, device_id_type=MESH)

    t_index = lax.broadcasted_iota(jnp.int32, (block, block), 0)
    s_index = lax.broadcasted_iota(jnp.int32, (block, block), 1)
    tri[...] = jnp.where(t_index >= s_index, 1.0, 0.0).astype(BF16)

    def parts(value):
        hi = value.astype(BF16)
        rest = value - hi.astype(F32)
        mid = rest.astype(BF16)
        return hi, mid, (rest - mid.astype(F32)).astype(BF16)

    for h in range(heads):
        total = None
        for part in parts(jnp.broadcast_to(ld_ref[0, h : h + 1, :], (hs, block))):
            term = lax.dot_general(tri[...], part, NT, preferred_element_type=F32)
            total = term if total is None else total + term
        col[h] = total
    rates = jnp.concatenate([ld_ref[0, 0:heads, :]] * (8 // heads), axis=0)
    row = None
    for part in parts(rates):
        term = lax.dot_general(part, tri[...], NT, preferred_element_type=F32)
        row = term if row is None else row + term

    loads[0].wait()
    loads[1].wait()
    v[...] = (cnt[...].astype(F32) * scale_ref[...]).astype(BF16)

    def decay_rows(decays):
        index = lax.broadcasted_iota(jnp.int32, (16, hs), 0)
        rows = jnp.zeros((16, hs), F32)
        for h, decay in enumerate(decays):
            hi = decay.astype(BF16).astype(F32)
            rows = jnp.where(index == 2 * h, hi, rows)
            rows = jnp.where(index == 2 * h + 1, decay - hi, rows)
        return rows.astype(BF16)

    def read_decays(tile):
        rows = tile.astype(F32)
        return [rows[2 * h : 2 * h + 1, :] + rows[2 * h + 1 : 2 * h + 2, :] for h in range(heads)]

    depth = heads * quarter
    own_decay = []
    for h in range(heads):
        lanes = slice(h * hs, (h + 1) * hs)
        last = col[h, block - 1 : block, :]
        to_end = jnp.exp(last - col[h])
        weighted = (k[:, lanes].astype(F32) * to_end).astype(BF16)
        state = lax.dot_general(weighted, v[:, lanes], TN, preferred_element_type=F32)
        for part in range(NX):
            p1_send[part, h * quarter : (h + 1) * quarter, :] = state[
                part * quarter : (part + 1) * quarter, :
            ].astype(BF16)
        own_decay.append(jnp.exp(last))
    own_rows = decay_rows(own_decay)
    for part in range(NX):
        p1_send[part, depth : depth + 16, :] = own_rows

    pl.semaphore_wait(barrier, len(friends))

    for d in (2, 1, 3):
        net.send(("p1", d), p1_send.at[xp(d)], p1_recv.at[x], at_x(d))
    p1_recv[pl.ds(x, 1)] = p1_send[pl.ds(x, 1)]

    def w_x(c, rows=slice(0, xr)):
        return w_all.at[c, pl.ds(rows.start, rows.stop - rows.start), :]

    def w_y(c, lo=xr, hi=wrows):
        return w_all.at[c, pl.ds(lo, hi - lo), :]

    def bundle(d, lo=0, hi=NX):
        return w_all.at[pl.ds(yp(d) * NX + lo, hi - lo), pl.ds(0, xr), :]

    x_lo, x_hi = slice(0, xr // 32 * 16), slice(xr // 32 * 16, xr)
    y_mid = xr + yr // 32 * 16

    def c_at(dy, dx):
        return yp(dy) * NX + xp(dx)

    def y1_send(step):
        if step < ry:
            net.send(("y1", step, 1), w_y(c_at(1 - step, 0)), w_y(c_at(1 - step, 0)), at_y(1))
            net.send(("y1", step, -1), w_y(c_at(step - 1, 0)), w_y(c_at(step - 1, 0)), at_y(-1))
        else:
            net.send(("y1", step, 1), w_y(c_at(1 - step, 0), xr, y_mid), w_y(c_at(1 - step, 0), xr, y_mid), at_y(1))
            net.send(("y1", step, -1), w_y(c_at(step - 1, 0), y_mid), w_y(c_at(step - 1, 0), y_mid), at_y(-1))

    def y1_wait(step):
        if step < ry:
            net.arrive(("y1", step, 1), w_y(c_at(-step, 0)), at_y(-1))
            net.arrive(("y1", step, -1), w_y(c_at(step, 0)), at_y(1))
        else:
            net.arrive(("y1", step, 1), w_y(c_at(-step, 0), xr, y_mid), at_y(-1))
            net.arrive(("y1", step, -1), w_y(c_at(step, 0), y_mid), at_y(1))

    def y2_send(d):
        for way in (1, -1):
            net.send(("y2", d, way), w_y(c_at(d, 0)), w_y(c_at(d, 0)), at_x(way))

    def y2_relay(d):
        for way in (1, -1):
            net.arrive(("y2", d, way), w_y(c_at(d, -way)), at_x(-way))
        way = 1 if 0 <= d < ry else -1
        net.send(("y3", d), w_y(c_at(d, -way)), w_y(c_at(d, -way)), at_x(way))

    def y3_wait(d):
        way = 1 if 0 <= d < ry else -1
        net.arrive(("y3", d), w_y(c_at(d, 2)), at_x(-way))

    def x1_send():
        for way in (1, -1):
            net.send(("x1", way), w_x(ctx), w_x(ctx), at_x(way))

    def x1_relay():
        for way in (1, -1):
            net.arrive(("x1", way), w_x(c_at(0, -way)), at_x(-way))
        for way, rows in ((1, x_lo), (-1, x_hi)):
            net.send(("x1r", way), w_x(c_at(0, -way), rows), w_x(c_at(0, -way), rows), at_x(way))

    def x1_wait():
        for way, rows in ((1, x_lo), (-1, x_hi)):
            net.arrive(("x1r", way), w_x(c_at(0, 2), rows), at_x(-way))

    def x2_range(step, way):
        if step < ry:
            return 0, NX
        return (0, NX // 2) if way == 1 else (NX // 2, NX)

    def x2_send(step):
        for way in (1, -1):
            part = bundle(way * (1 - step), *x2_range(step, way))
            net.send(("x2", step, way), part, part, at_y(way))

    def x2_wait(step):
        for way in (1, -1):
            net.arrive(("x2", step, way), bundle(-way * step, *x2_range(step, way)), at_y(-way))

    strip = block // 4
    s_in = lax.broadcasted_iota(jnp.int32, (strip, strip), 1)
    t_in = lax.broadcasted_iota(jnp.int32, (strip, strip), 0)

    def attend(h):
        lanes = slice(h * hs, (h + 1) * hs)
        for i in range(4):
            rows, upto = slice(i * strip, (i + 1) * strip), (i + 1) * strip
            scores = lax.dot_general(q[rows, lanes], k[0:upto, lanes], NT, preferred_element_type=F32)
            here = col[h, rows, 0:1]
            pieces = []
            for j in range(i + 1):
                gap = here - row[h : h + 1, j * strip : (j + 1) * strip]
                if j == i:
                    gap = jnp.where(t_in >= s_in, gap, -1e30)
                pieces.append((scores[:, j * strip : (j + 1) * strip] * jnp.exp(gap)).astype(BF16))
            weights = jnp.concatenate(pieces, axis=1) if i else pieces[0]
            intra[h, rows, :] = jnp.dot(weights, v[0:upto, lanes], preferred_element_type=F32)

    loads[2].wait()
    x1_send()
    y1_send(1)
    loads[3].wait()
    attend(0)

    for d in range(1, NX):
        net.arrive(("p1", d), p1_recv.at[xp(-d)], at_x(-d))
    inside, before = [], []
    run = [jnp.zeros((quarter, hs), F32) for _ in range(heads)]
    run_decay = [jnp.ones((1, hs), F32) for _ in range(heads)]
    for i in range(NX):
        inside.append(run)
        before.append(run_decay)
        decays = read_decays(p1_recv[i, depth : depth + 16, :])
        states = [p1_recv[i, h * quarter : (h + 1) * quarter, :].astype(F32) for h in range(heads)]
        run = [run[h] * decays[h] + states[h] for h in range(heads)]
        run_decay = [run_decay[h] * decays[h] for h in range(heads)]
    for h in range(heads):
        p2_send[h * quarter : (h + 1) * quarter, :] = run[h].astype(BF16)
    p2_send[depth : depth + 16, :] = decay_rows(run_decay)
    for d in sorted(range(1, ny), key=lambda d: -min(d, ny - d)):
        net.send(("p2", d), p2_send, p2_recv.at[d - 1], at_y(d), when=y + d < ny)

    x1_relay()
    y2_send(0)
    y1_wait(1)
    y2_send(1)
    y2_send(-1)
    attend(1)

    for d in range(1, ny):
        net.arrive(("p2", d), p2_recv.at[d - 1], at_y(-d), when=y >= d)
    rows_before = [jnp.zeros((quarter, hs), F32) for _ in range(heads)]
    for d in range(ny - 1, 0, -1):
        there = y >= d
        decays = read_decays(p2_recv[d - 1, depth : depth + 16, :])
        for h in range(heads):
            state = p2_recv[d - 1, h * quarter : (h + 1) * quarter, :].astype(F32)
            rows_before[h] = jnp.where(there, rows_before[h] * decays[h] + state, 0.0)
    for i in range(NX):
        for h in range(heads):
            p3_send[i, h * quarter : (h + 1) * quarter, :] = (
                rows_before[h] * before[i][h] + inside[i][h]
            ).astype(BF16)
    for d in (2, 1, 3):
        net.send(("p3", d), p3_send.at[xp(d)], p3_recv.at[x], at_x(d))
    p3_recv[pl.ds(x, 1)] = p3_send[pl.ds(x, 1)]
    y1_send(2)
    x1_wait()
    x2_send(1)
    y2_relay(0)

    for d in range(1, NX):
        net.arrive(("p3", d), p3_recv.at[xp(-d)], at_x(-d))

    def piece(t, part):
        return a_all.at[t, pl.ds(part * half, half), :]

    def z_item(i, way):
        return -way * (i // 2), (i % 2 if way == 1 else 1 - i % 2)

    def z_send(i, way):
        d, part = z_item(i, way)
        own = piece(zp(d) * 2 + core, part)
        net.send(("z", i, way), own, own, at_z(way))

    def z_wait(i, way):
        d, part = z_item(i, way)
        net.arrive(("z", i, way), piece(zp(d - way) * 2 + core, part), at_z(-way))

    def hand(d, part):
        own = piece(zp(d) * 2 + core, part)
        net.send(("hand", d, part), own, own, partner)

    def hand_wait(d, part):
        net.arrive(("hand", d, part), piece(zp(d) * 2 + (1 - core), part), partner)

    incoming = [
        jnp.concatenate([p3_recv[i, h * quarter : (h + 1) * quarter, :] for i in range(NX)], axis=0)
        for h in range(heads)
    ]
    for part in range(2):
        rows = slice(part * half, (part + 1) * half)
        for h in range(heads):
            lanes = slice(h * hs, (h + 1) * hs)
            carried = jnp.dot(q[rows, lanes], incoming[h], preferred_element_type=F32)
            mixed = intra[h, rows, :] + jnp.exp(col[h, rows, :]) * carried
            scale = lax.rsqrt(jnp.mean(mixed * mixed, axis=1, keepdims=True) + EPSILON)
            a_all[ten, rows, lanes] = (mixed * scale * gain_ref[:, lanes]).astype(BF16)
        z_send(part, 1)
        z_send(1 - part, -1) if part else None
    z_send(1, -1)
    hand(0, 0)
    hand(0, 1)

    w_events = [
        [lambda: y1_wait(2), lambda: y1_send(3), lambda: y2_send(2), lambda: y2_send(-2),
         lambda: y2_relay(1), lambda: y2_relay(-1), lambda: x2_wait(1), lambda: x2_send(2)],
        [lambda: y1_wait(3), lambda: y1_send(4), lambda: y2_send(3), lambda: y2_send(-3),
         lambda: y2_relay(2), lambda: y2_relay(-2), lambda: x2_wait(2), lambda: x2_send(3)],
        [lambda: y1_wait(4), lambda: y2_send(4), lambda: y2_relay(3), lambda: y2_relay(-3),
         lambda: x2_wait(3), lambda: x2_send(4)],
        [lambda: y2_relay(4)],
        [lambda: x2_wait(4)] + [functools.partial(y3_wait, d) for d in (0, 1, -1, 2, -2, 3, -3, 4)],
    ]

    def multiply(d, part, first=False):
        rows = pl.ds(part * half, half)
        base = zp(d)
        result = None
        for c in range(2):
            weight = w_all[pl.ds(base * 4 + 2 * c, 2)].reshape(2 * wrows, -1)
            term = jnp.dot(a_all[base * 2 + c, rows, :], weight, preferred_element_type=F32)
            result = term if result is None else result + term
        if first:
            acc[rows, :] = result
        else:
            acc[rows, :] += result

    last = 2 * rz - 2
    for i in range(last + 1):
        for way in (1, -1):
            z_wait(i, way)
            if i + 2 <= last:
                z_send(i + 2, way)
            d, part = z_item(i, way)
            hand(d - way, part)
        if i < len(w_events):
            for event in w_events[i]:
                event()
        if i == 4:
            hand_wait(0, 0)
            hand_wait(0, 1)
            multiply(0, 0, True)
            multiply(0, 1, True)
            for d in (-1, 1, -2, 2):
                for part in range(2):
                    hand_wait(d, part)
                    multiply(d, part)
        if i == 5:
            for d in (-3, 3):
                for part in range(2):
                    hand_wait(d, part)
                    multiply(d, part)
    loads[4].wait()
    stores = []
    for part in range(2):
        rows = pl.ds(part * half, half)
        d = -4 if part == 0 else 4
        hand_wait(d, part)
        multiply(d, part)
        out[rows, :] = (res[rows, :].astype(F32) + acc[rows, :]).astype(BF16)
        stores.append(pltpu.make_async_copy(out.at[rows, :], out_hbm.at[0, rows, :], load_sem.at[5 + part]))
        stores[-1].start()
    for store in stores:
        store.wait()
    net.drain()


def local(dims, queries, keys, spike_counts, spike_scale, log_decay, norm_gain, out_weight, residual_in):
    ny, nz, heads, hs, block, wrows, xr = dims
    width = heads * hs
    columns = out_weight.shape[1]
    depth = heads * hs // NX + 16
    vmem = pl.BlockSpec(memory_space=pltpu.VMEM)
    hbm = pl.BlockSpec(memory_space=pl.ANY)
    return pl.pallas_call(
        functools.partial(kernel, dims),
        out_shape=jax.ShapeDtypeStruct((1, block, columns), BF16),
        in_specs=[hbm, hbm, hbm, vmem, vmem, vmem, hbm, hbm],
        out_specs=hbm,
        scratch_shapes=[
            pltpu.VMEM((block, width), BF16),
            pltpu.VMEM((block, width), BF16),
            pltpu.VMEM((block, width), jnp.int32),
            pltpu.VMEM((block, columns), BF16),
            pltpu.VMEM((block, width), BF16),
            pltpu.VMEM((block, columns), F32),
            pltpu.VMEM((block, columns), BF16),
            pltpu.VMEM((block, block), BF16),
            pltpu.VMEM((heads, block, hs), F32),
            pltpu.VMEM((heads, block, hs), F32),
            pltpu.VMEM((2 * nz, block, width), BF16),
            pltpu.VMEM((ny * NX, wrows, columns), BF16),
            pltpu.VMEM((NX, depth, hs), BF16),
            pltpu.VMEM((NX, depth, hs), BF16),
            pltpu.VMEM((depth, hs), BF16),
            pltpu.VMEM((ny - 1, depth, hs), BF16),
            pltpu.VMEM((NX, depth - 16, hs), BF16),
            pltpu.VMEM((NX, depth - 16, hs), BF16),
            pltpu.SemaphoreType.DMA((96,)),
            pltpu.SemaphoreType.DMA((96,)),
            pltpu.SemaphoreType.DMA((8,)),
        ],
        compiler_params=pltpu.CompilerParams(
            collective_id=0, has_side_effects=True, vmem_limit_bytes=40 * 1024 * 1024
        ),
    )(
        queries, keys, spike_counts, spike_scale.reshape(1, width), log_decay,
        norm_gain.reshape(1, width), out_weight, residual_in,
    )


def solution(mesh):
    ny, nz = mesh.shape["context"] // NX, mesh.shape["tensor"] // 2

    def whole(queries, keys, spike_counts, spike_scale, log_decay, norm_gain, out_weight, residual_in):
        heads = log_decay.shape[1] // (2 * nz)
        hs = queries.shape[2] // log_decay.shape[1]
        block = queries.shape[1] // (ny * NX)
        wrows = out_weight.shape[0] // (ny * NX)
        xr = wrows * 3 // 8
        dims = (ny, nz, heads, hs, block, wrows, xr)
        in_specs = (
            P(None, "context", "tensor"),
            P(None, "context", "tensor"),
            P(None, "context", "tensor"),
            P("tensor"),
            P(None, "tensor", "context"),
            P("tensor"),
            P("context", "tensor"),
            P(None, "context", "tensor"),
        )
        return jax.shard_map(
            functools.partial(local, dims),
            mesh=mesh,
            in_specs=in_specs,
            out_specs=P(None, "context", "tensor"),
            check_vma=False,
        )(queries, keys, spike_counts, spike_scale, log_decay, norm_gain, out_weight, residual_in)

    return whole
```

```python
import functools

import jax
import jax.numpy as jnp
from jax import lax
from jax.experimental import pallas as pl
from jax.experimental.pallas import tpu as pltpu
from jax.sharding import PartitionSpec as P

MESH = pl.DeviceIdType.MESH
NX = 4
EPSILON = 1e-06
F32 = jnp.float32
BF16 = jnp.bfloat16
NT = (((1,), (1,)), ((), ()))
TN = (((0,), (0,)), ((), ()))


class Net:
    def __init__(self, send_sem, recv_sem):
        self.send_sem, self.recv_sem = send_sem, recv_sem
        self.number = {}
        self.sent = []

    def slot(self, name):
        return self.number.setdefault(name, len(self.number))

    def copy(self, name, src, dst, target):
        i = self.slot(name)
        return pltpu.make_async_remote_copy(
            src_ref=src,
            dst_ref=dst,
            send_sem=self.send_sem.at[i],
            recv_sem=self.recv_sem.at[i],
            device_id=target,
            device_id_type=MESH,
        )

    def send(self, name, src, dst, target, when=None):
        copy = self.copy(name, src, dst, target)
        if when is None:
            copy.start()
        else:
            pl.when(when)(copy.start)
        self.sent.append((copy, when))

    def arrive(self, name, place, source, when=None):
        copy = self.copy(name, place, place, source)
        if when is None:
            copy.wait_recv()
        else:
            pl.when(when)(copy.wait_recv)

    def drain(self):
        for copy, when in self.sent:
            if when is None:
                copy.wait_send()
            else:
                pl.when(when)(copy.wait_send)


def kernel(
    dims,
    q_hbm, k_hbm, cnt_hbm, scale_hbm, ld_hbm, gain_hbm, w_hbm, res_hbm, out_ref,
    q, k, cnt, scale_ref, ld_ref, gain_ref, res, v, acc, tri, col, intra, a_all, w_all,
    p1_send, p1_recv, p2_send, p2_recv, p3_send, p3_recv,
    send_sem, recv_sem, load_sem,
):
    ny, nz, heads, hs, block, wrows, xr = dims
    ctx, ten = lax.axis_index("context"), lax.axis_index("tensor")
    y, x = ctx // NX, ctx % NX
    z, core = ten // 2, ten % 2
    quarter = hs // NX
    half = block // 2
    ry, rz = ny // 2, nz // 2
    yr = wrows - xr

    def yp(d):
        return lax.rem(y + (d + ny), ny)

    def xp(d):
        return lax.rem(x + (d + NX), NX)

    def zp(d):
        return lax.rem(z + (d + nz), nz)

    def at_y(d):
        return (yp(d) * NX + x, ten)

    def at_x(d):
        return (y * NX + xp(d), ten)

    def at_z(d):
        return (ctx, zp(d) * 2 + core)

    partner = (ctx, z * 2 + (1 - core))
    net = Net(send_sem, recv_sem)

    loads = [
        pltpu.make_async_copy(k_hbm.at[0], k, load_sem.at[0]),
        pltpu.make_async_copy(cnt_hbm.at[0], cnt, load_sem.at[1]),
        pltpu.make_async_copy(w_hbm, w_all.at[ctx], load_sem.at[2]),
        pltpu.make_async_copy(q_hbm.at[0], q, load_sem.at[3]),
        pltpu.make_async_copy(res_hbm.at[0], res, load_sem.at[4]),
        pltpu.make_async_copy(ld_hbm, ld_ref, load_sem.at[5]),
        pltpu.make_async_copy(scale_hbm, scale_ref, load_sem.at[6]),
        pltpu.make_async_copy(gain_hbm, gain_ref, load_sem.at[7]),
    ]
    for i in (5, 6, 0, 1, 2, 3, 7, 4):
        loads[i].start()
    barrier = pltpu.get_barrier_semaphore()
    friends = [at_y(d) for d in range(1, ny)] + [at_x(d) for d in range(1, NX)]
    friends += [at_z(1), at_z(-1), partner]
    for friend in friends:
        pl.semaphore_signal(barrier, inc=1, device_id=friend, device_id_type=MESH)

    t_index = lax.broadcasted_iota(jnp.int32, (block, block), 0)
    s_index = lax.broadcasted_iota(jnp.int32, (block, block), 1)
    tri[...] = jnp.where(t_index >= s_index, 1.0, 0.0).astype(BF16)

    def parts(value):
        hi = value.astype(BF16)
        rest = value - hi.astype(F32)
        mid = rest.astype(BF16)
        return hi, mid, (rest - mid.astype(F32)).astype(BF16)

    loads[5].wait()
    for h in range(heads):
        total = None
        for part in parts(jnp.broadcast_to(ld_ref[0, h : h + 1, :], (hs, block))):
            term = lax.dot_general(tri[...], part, NT, preferred_element_type=F32)
            total = term if total is None else total + term
        col[h] = total
    rates = jnp.concatenate([ld_ref[0, 0:heads, :]] * (8 // heads), axis=0)
    row = None
    for part in parts(rates):
        term = lax.dot_general(part, tri[...], NT, preferred_element_type=F32)
        row = term if row is None else row + term

    loads[0].wait()
    loads[1].wait()
    loads[6].wait()
    v[...] = (cnt[...].astype(F32) * scale_ref[...]).astype(BF16)

    def decay_rows(decays):
        index = lax.broadcasted_iota(jnp.int32, (16, hs), 0)
        rows = jnp.zeros((16, hs), F32)
        for h, decay in enumerate(decays):
            hi = decay.astype(BF16).astype(F32)
            rows = jnp.where(index == 2 * h, hi, rows)
            rows = jnp.where(index == 2 * h + 1, decay - hi, rows)
        return rows.astype(BF16)

    def read_decays(tile):
        rows = tile.astype(F32)
        return [rows[2 * h : 2 * h + 1, :] + rows[2 * h + 1 : 2 * h + 2, :] for h in range(heads)]

    depth = heads * quarter
    own_decay = []
    for h in range(heads):
        lanes = slice(h * hs, (h + 1) * hs)
        last = col[h, block - 1 : block, :]
        to_end = jnp.exp(last - col[h])
        weighted = (k[:, lanes].astype(F32) * to_end).astype(BF16)
        state = lax.dot_general(weighted, v[:, lanes], TN, preferred_element_type=F32)
        for part in range(NX):
            p1_send[part, h * quarter : (h + 1) * quarter, :] = state[
                part * quarter : (part + 1) * quarter, :
            ].astype(BF16)
        own_decay.append(jnp.exp(last))
    own_rows = decay_rows(own_decay)
    for part in range(NX):
        p1_send[part, depth : depth + 16, :] = own_rows

    pl.semaphore_wait(barrier, len(friends))

    for d in (2, 1, 3):
        net.send(("p1", d), p1_send.at[xp(d)], p1_recv.at[x], at_x(d))
    p1_recv[pl.ds(x, 1)] = p1_send[pl.ds(x, 1)]

    def w_x(c, rows=slice(0, xr)):
        return w_all.at[c, pl.ds(rows.start, rows.stop - rows.start), :]

    def w_y(c, lo=xr, hi=wrows):
        return w_all.at[c, pl.ds(lo, hi - lo), :]

    def bundle(d, lo=0, hi=NX):
        return w_all.at[pl.ds(yp(d) * NX + lo, hi - lo), pl.ds(0, xr), :]

    x_lo, x_hi = slice(0, xr // 32 * 16), slice(xr // 32 * 16, xr)
    y_mid = xr + yr // 32 * 16

    def c_at(dy, dx):
        return yp(dy) * NX + xp(dx)

    def y1_send(step):
        if step < ry:
            net.send(("y1", step, 1), w_y(c_at(1 - step, 0)), w_y(c_at(1 - step, 0)), at_y(1))
            net.send(("y1", step, -1), w_y(c_at(step - 1, 0)), w_y(c_at(step - 1, 0)), at_y(-1))
        else:
            net.send(("y1", step, 1), w_y(c_at(1 - step, 0), xr, y_mid), w_y(c_at(1 - step, 0), xr, y_mid), at_y(1))
            net.send(("y1", step, -1), w_y(c_at(step - 1, 0), y_mid), w_y(c_at(step - 1, 0), y_mid), at_y(-1))

    def y1_wait(step):
        if step < ry:
            net.arrive(("y1", step, 1), w_y(c_at(-step, 0)), at_y(-1))
            net.arrive(("y1", step, -1), w_y(c_at(step, 0)), at_y(1))
        else:
            net.arrive(("y1", step, 1), w_y(c_at(-step, 0), xr, y_mid), at_y(-1))
            net.arrive(("y1", step, -1), w_y(c_at(step, 0), y_mid), at_y(1))

    def y2_send(d):
        for way in (1, -1):
            net.send(("y2", d, way), w_y(c_at(d, 0)), w_y(c_at(d, 0)), at_x(way))

    def y2_relay(d):
        for way in (1, -1):
            net.arrive(("y2", d, way), w_y(c_at(d, -way)), at_x(-way))
        way = 1 if 0 <= d < ry else -1
        net.send(("y3", d), w_y(c_at(d, -way)), w_y(c_at(d, -way)), at_x(way))

    def y3_wait(d):
        way = 1 if 0 <= d < ry else -1
        net.arrive(("y3", d), w_y(c_at(d, 2)), at_x(-way))

    def x1_send():
        for way in (1, -1):
            net.send(("x1", way), w_x(ctx), w_x(ctx), at_x(way))

    def x1_relay():
        for way in (1, -1):
            net.arrive(("x1", way), w_x(c_at(0, -way)), at_x(-way))
        for way, rows in ((1, x_lo), (-1, x_hi)):
            net.send(("x1r", way), w_x(c_at(0, -way), rows), w_x(c_at(0, -way), rows), at_x(way))

    def x1_wait():
        for way, rows in ((1, x_lo), (-1, x_hi)):
            net.arrive(("x1r", way), w_x(c_at(0, 2), rows), at_x(-way))

    def x2_range(step, way):
        if step < ry:
            return 0, NX
        return (0, NX // 2) if way == 1 else (NX // 2, NX)

    def x2_send(step):
        for way in (1, -1):
            part = bundle(way * (1 - step), *x2_range(step, way))
            net.send(("x2", step, way), part, part, at_y(way))

    def x2_wait(step):
        for way in (1, -1):
            net.arrive(("x2", step, way), bundle(-way * step, *x2_range(step, way)), at_y(-way))

    strip = block // 4
    s_in = lax.broadcasted_iota(jnp.int32, (strip, strip), 1)
    t_in = lax.broadcasted_iota(jnp.int32, (strip, strip), 0)

    def attend(h):
        lanes = slice(h * hs, (h + 1) * hs)
        for i in range(4):
            rows, upto = slice(i * strip, (i + 1) * strip), (i + 1) * strip
            scores = lax.dot_general(q[rows, lanes], k[0:upto, lanes], NT, preferred_element_type=F32)
            here = col[h, rows, 0:1]
            pieces = []
            for j in range(i + 1):
                gap = here - row[h : h + 1, j * strip : (j + 1) * strip]
                if j == i:
                    gap = jnp.where(t_in >= s_in, gap, -1e30)
                pieces.append((scores[:, j * strip : (j + 1) * strip] * jnp.exp(gap)).astype(BF16))
            weights = jnp.concatenate(pieces, axis=1) if i else pieces[0]
            intra[h, rows, :] = jnp.dot(weights, v[0:upto, lanes], preferred_element_type=F32)

    loads[2].wait()
    x1_send()
    y1_send(1)
    loads[3].wait()
    attend(0)

    for d in range(1, NX):
        net.arrive(("p1", d), p1_recv.at[xp(-d)], at_x(-d))
    inside, before = [], []
    run = [jnp.zeros((quarter, hs), F32) for _ in range(heads)]
    run_decay = [jnp.ones((1, hs), F32) for _ in range(heads)]
    for i in range(NX):
        inside.append(run)
        before.append(run_decay)
        decays = read_decays(p1_recv[i, depth : depth + 16, :])
        states = [p1_recv[i, h * quarter : (h + 1) * quarter, :].astype(F32) for h in range(heads)]
        run = [run[h] * decays[h] + states[h] for h in range(heads)]
        run_decay = [run_decay[h] * decays[h] for h in range(heads)]
    for h in range(heads):
        p2_send[h * quarter : (h + 1) * quarter, :] = run[h].astype(BF16)
    p2_send[depth : depth + 16, :] = decay_rows(run_decay)
    for d in sorted(range(1, ny), key=lambda d: -min(d, ny - d)):
        net.send(("p2", d), p2_send, p2_recv.at[d - 1], at_y(d), when=y + d < ny)

    x1_relay()
    y2_send(0)
    y1_wait(1)
    y2_send(1)
    y2_send(-1)
    attend(1)

    for d in range(1, ny):
        net.arrive(("p2", d), p2_recv.at[d - 1], at_y(-d), when=y >= d)
    rows_before = [jnp.zeros((quarter, hs), F32) for _ in range(heads)]
    for d in range(ny - 1, 0, -1):
        there = y >= d
        decays = read_decays(p2_recv[d - 1, depth : depth + 16, :])
        for h in range(heads):
            state = p2_recv[d - 1, h * quarter : (h + 1) * quarter, :].astype(F32)
            rows_before[h] = jnp.where(there, rows_before[h] * decays[h] + state, 0.0)
    for i in range(NX):
        for h in range(heads):
            p3_send[i, h * quarter : (h + 1) * quarter, :] = (
                rows_before[h] * before[i][h] + inside[i][h]
            ).astype(BF16)
    for d in (2, 1, 3):
        net.send(("p3", d), p3_send.at[xp(d)], p3_recv.at[x], at_x(d))
    p3_recv[pl.ds(x, 1)] = p3_send[pl.ds(x, 1)]
    y1_send(2)
    x1_wait()
    x2_send(1)
    y2_relay(0)

    for d in range(1, NX):
        net.arrive(("p3", d), p3_recv.at[xp(-d)], at_x(-d))

    def piece(t, part):
        return a_all.at[t, pl.ds(part * half, half), :]

    def z_item(i, way):
        return -way * (i // 2), (i % 2 if way == 1 else 1 - i % 2)

    def z_send(i, way):
        d, part = z_item(i, way)
        own = piece(zp(d) * 2 + core, part)
        net.send(("z", i, way), own, own, at_z(way))

    def z_wait(i, way):
        d, part = z_item(i, way)
        net.arrive(("z", i, way), piece(zp(d - way) * 2 + core, part), at_z(-way))

    def hand(d, part):
        own = piece(zp(d) * 2 + core, part)
        net.send(("hand", d, part), own, own, partner)

    def hand_wait(d, part):
        net.arrive(("hand", d, part), piece(zp(d) * 2 + (1 - core), part), partner)

    incoming = [
        jnp.concatenate([p3_recv[i, h * quarter : (h + 1) * quarter, :] for i in range(NX)], axis=0)
        for h in range(heads)
    ]
    loads[7].wait()
    for part in range(2):
        rows = slice(part * half, (part + 1) * half)
        for h in range(heads):
            lanes = slice(h * hs, (h + 1) * hs)
            carried = jnp.dot(q[rows, lanes], incoming[h], preferred_element_type=F32)
            mixed = intra[h, rows, :] + jnp.exp(col[h, rows, :]) * carried
            scale = lax.rsqrt(jnp.mean(mixed * mixed, axis=1, keepdims=True) + EPSILON)
            a_all[ten, rows, lanes] = (mixed * scale * gain_ref[:, lanes]).astype(BF16)
        z_send(part, 1)
        z_send(1 - part, -1) if part else None
    z_send(1, -1)
    hand(0, 0)
    hand(0, 1)

    w_events = [
        [lambda: y1_wait(2), lambda: y1_send(3), lambda: y2_send(2), lambda: y2_send(-2),
         lambda: y2_relay(1), lambda: y2_relay(-1), lambda: x2_wait(1), lambda: x2_send(2)],
        [lambda: y1_wait(3), lambda: y1_send(4), lambda: y2_send(3), lambda: y2_send(-3),
         lambda: y2_relay(2), lambda: y2_relay(-2), lambda: x2_wait(2), lambda: x2_send(3)],
        [lambda: y1_wait(4), lambda: y2_send(4), lambda: y2_relay(3), lambda: y2_relay(-3),
         lambda: x2_wait(3), lambda: x2_send(4)],
        [lambda: y2_relay(4)],
        [lambda: x2_wait(4)] + [functools.partial(y3_wait, d) for d in (0, 1, -1, 2, -2, 3, -3, 4)],
    ]

    def multiply(d, part, first=False):
        rows = pl.ds(part * half, half)
        base = zp(d)
        result = None
        for c in range(2):
            weight = w_all[pl.ds(base * 4 + 2 * c, 2)].reshape(2 * wrows, -1)
            term = jnp.dot(a_all[base * 2 + c, rows, :], weight, preferred_element_type=F32)
            result = term if result is None else result + term
        if first:
            acc[rows, :] = result
        else:
            acc[rows, :] += result

    last = 2 * rz - 2
    for i in range(last + 1):
        for way in (1, -1):
            z_wait(i, way)
            if i + 2 <= last:
                z_send(i + 2, way)
            d, part = z_item(i, way)
            hand(d - way, part)
        if i < len(w_events):
            for event in w_events[i]:
                event()
        if i == 4:
            hand_wait(0, 0)
            hand_wait(0, 1)
            multiply(0, 0, True)
            multiply(0, 1, True)
            for d in (-1, 1, -2, 2):
                for part in range(2):
                    hand_wait(d, part)
                    multiply(d, part)
        if i == 5:
            for d in (-3, 3):
                for part in range(2):
                    hand_wait(d, part)
                    multiply(d, part)
    loads[4].wait()
    for part in range(2):
        rows = pl.ds(part * half, half)
        d = -4 if part == 0 else 4
        hand_wait(d, part)
        multiply(d, part)
        out_ref[0, rows, :] = (res[rows, :].astype(F32) + acc[rows, :]).astype(BF16)
    net.drain()


def local(dims, queries, keys, spike_counts, spike_scale, log_decay, norm_gain, out_weight, residual_in):
    ny, nz, heads, hs, block, wrows, xr = dims
    width = heads * hs
    columns = out_weight.shape[1]
    depth = heads * hs // NX + 16
    vmem = pl.BlockSpec(memory_space=pltpu.VMEM)
    hbm = pl.BlockSpec(memory_space=pltpu.HBM)
    return pl.pallas_call(
        functools.partial(kernel, dims),
        out_shape=pltpu.VMEM((1, block, columns), BF16),
        in_specs=[hbm] * 8,
        out_specs=vmem,
        scratch_shapes=[
            pltpu.VMEM((block, width), BF16),
            pltpu.VMEM((block, width), BF16),
            pltpu.VMEM((block, width), jnp.int32),
            pltpu.VMEM((1, width), F32),
            pltpu.VMEM((1, heads, block), F32),
            pltpu.VMEM((1, width), F32),
            pltpu.VMEM((block, columns), BF16),
            pltpu.VMEM((block, width), BF16),
            pltpu.VMEM((block, columns), F32),
            pltpu.VMEM((block, block), BF16),
            pltpu.VMEM((heads, block, hs), F32),
            pltpu.VMEM((heads, block, hs), F32),
            pltpu.VMEM((2 * nz, block, width), BF16),
            pltpu.VMEM((ny * NX, wrows, columns), BF16),
            pltpu.VMEM((NX, depth, hs), BF16),
            pltpu.VMEM((NX, depth, hs), BF16),
            pltpu.VMEM((depth, hs), BF16),
            pltpu.VMEM((ny - 1, depth, hs), BF16),
            pltpu.VMEM((NX, depth - 16, hs), BF16),
            pltpu.VMEM((NX, depth - 16, hs), BF16),
            pltpu.SemaphoreType.DMA((96,)),
            pltpu.SemaphoreType.DMA((96,)),
            pltpu.SemaphoreType.DMA((8,)),
        ],
        compiler_params=pltpu.CompilerParams(
            collective_id=0, has_side_effects=True, vmem_limit_bytes=60 * 1024 * 1024
        ),
    )(
        queries, keys, spike_counts, spike_scale.reshape(1, width), log_decay,
        norm_gain.reshape(1, width), out_weight, residual_in,
    )


def solution(mesh):
    ny, nz = mesh.shape["context"] // NX, mesh.shape["tensor"] // 2

    def whole(queries, keys, spike_counts, spike_scale, log_decay, norm_gain, out_weight, residual_in):
        heads = log_decay.shape[1] // (2 * nz)
        hs = queries.shape[2] // log_decay.shape[1]
        block = queries.shape[1] // (ny * NX)
        wrows = out_weight.shape[0] // (ny * NX)
        xr = wrows * 3 // 8
        dims = (ny, nz, heads, hs, block, wrows, xr)
        in_specs = (
            P(None, "context", "tensor"),
            P(None, "context", "tensor"),
            P(None, "context", "tensor"),
            P("tensor"),
            P(None, "tensor", "context"),
            P("tensor"),
            P("context", "tensor"),
            P(None, "context", "tensor"),
        )
        return jax.shard_map(
            functools.partial(local, dims),
            mesh=mesh,
            in_specs=in_specs,
            out_specs=P(None, "context", "tensor"),
            check_vma=False,
        )(queries, keys, spike_counts, spike_scale, log_decay, norm_gain, out_weight, residual_in)

    return whole
```

```python
import functools

import jax
import jax.numpy as jnp
from jax import lax
from jax.experimental import pallas as pl
from jax.experimental.pallas import tpu as pltpu
from jax.sharding import PartitionSpec as P

MESH = pl.DeviceIdType.MESH
NX = 4
EPSILON = 1e-06
F32 = jnp.float32
BF16 = jnp.bfloat16
NT = (((1,), (1,)), ((), ()))
TN = (((0,), (0,)), ((), ()))


BEFORE_INCOMING = (
    ("x1", 1), ("x1", -1), ("y1", 1, 1), ("y1", 1, -1), ("s2", 1), ("s2", -1), ("x1r", 1), ("x1r", -1),
)
BEFORE_MIXED = (
    ("y2", 0, -1), ("y2", 0, 1), ("y1", 2, 1), ("y1", 2, -1), ("y2", 1, 1), ("y2", 1, -1), ("s2", -2), ("s2", 2),
    ("y2", -1, 1), ("y2", -1, -1),
)
AFTER_MIXED = (
    ("y3", 0), ("y2", -2, -1), ("x2", 1, -1), ("x2", 1, 1), ("y3", 1), ("y2", 2, -1), ("y1", 3, -1), ("s2", 3),
    ("y1", 3, 1), ("s2", -3), ("y2", -2, 1), ("y3", -1), ("z", 0, -1), ("z", 0, 1), ("y2", 2, 1), ("y3", -2),
    ("x2", 2, -1), ("x2", 2, 1), ("z", 1, -1), ("z", 1, 1), ("y2", 3, 1), ("y1", 4, 1), ("y2", 3, -1), ("y1", 4, -1),
    ("s2", 4), ("y2", -3, 1), ("y2", -3, -1), ("z", 2, -1), ("z", 2, 1), ("y3", 2), ("y2", 4, -1), ("y3", 3),
    ("x2", 3, -1), ("z", 3, -1), ("z", 3, 1), ("x2", 3, 1), ("y3", -3), ("y2", 4, 1), ("y3", 4), ("z", 4, -1),
    ("z", 4, 1), ("x2", 4, -1), ("x2", 4, 1), ("z", 5, -1), ("z", 5, 1),
)


class Net:
    def __init__(self, send_sem, recv_sem):
        self.send_sem, self.recv_sem = send_sem, recv_sem
        self.number = {}
        self.sent = []

    def slot(self, name):
        return self.number.setdefault(name, len(self.number))

    def copy(self, name, src, dst, target):
        i = self.slot(name)
        return pltpu.make_async_remote_copy(
            src_ref=src,
            dst_ref=dst,
            send_sem=self.send_sem.at[i],
            recv_sem=self.recv_sem.at[i],
            device_id=target,
            device_id_type=MESH,
        )

    def send(self, name, src, dst, target, when=None):
        copy = self.copy(name, src, dst, target)
        if when is None:
            copy.start()
        else:
            pl.when(when)(copy.start)
        self.sent.append((copy, when))

    def arrive(self, name, place, source, when=None):
        copy = self.copy(name, place, place, source)
        if when is None:
            copy.wait_recv()
        else:
            pl.when(when)(copy.wait_recv)

    def drain(self):
        for copy, when in self.sent:
            if when is None:
                copy.wait_send()
            else:
                pl.when(when)(copy.wait_send)


def kernel(
    dims,
    q_hbm, k_hbm, cnt_hbm, scale_hbm, ld_hbm, gain_hbm, w_hbm, res_hbm, out_ref,
    q, k, cnt, scale_ref, ld_ref, gain_ref, res, v, acc, col, intra, a_all, w_all,
    p1_send, p1_recv, p2_send, p2_recv, p3_send, p3_recv,
    send_sem, recv_sem, load_sem,
):
    ny, nz, heads, hs, block, wrows, xr = dims
    ctx, ten = lax.axis_index("context"), lax.axis_index("tensor")
    y, x = ctx // NX, ctx % NX
    z, core = ten // 2, ten % 2
    quarter = hs // NX
    half = block // 2
    ry, rz = ny // 2, nz // 2
    yr = wrows - xr

    def yp(d):
        return lax.rem(y + (d + ny), ny)

    def xp(d):
        return lax.rem(x + (d + NX), NX)

    def zp(d):
        return lax.rem(z + (d + nz), nz)

    def at_y(d):
        return (yp(d) * NX + x, ten)

    def at_x(d):
        return (y * NX + xp(d), ten)

    def at_z(d):
        return (ctx, zp(d) * 2 + core)

    partner = (ctx, z * 2 + (1 - core))
    net = Net(send_sem, recv_sem)

    loads = [
        pltpu.make_async_copy(k_hbm.at[0], k, load_sem.at[0]),
        pltpu.make_async_copy(cnt_hbm.at[0], cnt, load_sem.at[1]),
        pltpu.make_async_copy(w_hbm, w_all.at[ctx], load_sem.at[2]),
        pltpu.make_async_copy(q_hbm.at[0], q, load_sem.at[3]),
        pltpu.make_async_copy(res_hbm.at[0], res, load_sem.at[4]),
        pltpu.make_async_copy(ld_hbm, ld_ref, load_sem.at[5]),
        pltpu.make_async_copy(scale_hbm, scale_ref, load_sem.at[6]),
        pltpu.make_async_copy(gain_hbm, gain_ref, load_sem.at[7]),
    ]
    for i in (5, 6, 0, 1, 2, 3, 7, 4):
        loads[i].start()
    barrier = pltpu.get_barrier_semaphore()
    friends = [at_y(d) for d in range(1, ny)] + [at_x(d) for d in range(1, NX)]
    friends += [at_z(1), at_z(-1), partner]
    for friend in friends:
        pl.semaphore_signal(barrier, inc=1, device_id=friend, device_id_type=MESH)

    strip = block // 4
    t_in = lax.broadcasted_iota(jnp.int32, (strip, strip), 0)
    s_in = lax.broadcasted_iota(jnp.int32, (strip, strip), 1)
    tri = jnp.where(t_in >= s_in, 1.0, 0.0).astype(BF16)

    def parts(value):
        hi = value.astype(BF16)
        rest = value - hi.astype(F32)
        mid = rest.astype(BF16)
        return hi, mid, (rest - mid.astype(F32)).astype(BF16)

    loads[5].wait()
    row = []
    for h in range(heads):
        base, pieces = None, []
        for i in range(4):
            rates = ld_ref[0, h : h + 1, i * strip : (i + 1) * strip]
            down = along = None
            for part in parts(jnp.broadcast_to(rates, (hs, strip))):
                term = lax.dot_general(tri, part, NT, preferred_element_type=F32)
                down = term if down is None else down + term
                term = lax.dot_general(part[0:16], tri, NT, preferred_element_type=F32)
                along = term if along is None else along + term
            if i:
                down, along = down + base, along + base
            col[h, i * strip : (i + 1) * strip, :] = down
            base = down[strip - 1 : strip, :]
            pieces.append(along[0:1, :])
        row.append(jnp.concatenate(pieces, axis=1))

    loads[0].wait()
    loads[1].wait()
    loads[6].wait()
    v[...] = (cnt[...].astype(F32) * scale_ref[...]).astype(BF16)

    def decay_rows(decays):
        index = lax.broadcasted_iota(jnp.int32, (16, hs), 0)
        rows = jnp.zeros((16, hs), F32)
        for h, decay in enumerate(decays):
            hi = decay.astype(BF16).astype(F32)
            rows = jnp.where(index == 2 * h, hi, rows)
            rows = jnp.where(index == 2 * h + 1, decay - hi, rows)
        return rows.astype(BF16)

    def read_decays(tile):
        rows = tile.astype(F32)
        return [rows[2 * h : 2 * h + 1, :] + rows[2 * h + 1 : 2 * h + 2, :] for h in range(heads)]

    depth = heads * quarter
    own_decay = []
    for h in range(heads):
        lanes = slice(h * hs, (h + 1) * hs)
        last = col[h, block - 1 : block, :]
        to_end = jnp.exp(last - col[h])
        weighted = (k[:, lanes].astype(F32) * to_end).astype(BF16)
        state = lax.dot_general(weighted, v[:, lanes], TN, preferred_element_type=F32)
        for part in range(NX):
            p1_send[part, h * quarter : (h + 1) * quarter, :] = state[
                part * quarter : (part + 1) * quarter, :
            ].astype(BF16)
        own_decay.append(jnp.exp(last))
    own_rows = decay_rows(own_decay)
    for part in range(NX):
        p1_send[part, depth : depth + 16, :] = own_rows

    pl.semaphore_wait(barrier, len(friends))

    for d in (2, 1, 3):
        net.send(("p1", d), p1_send.at[xp(d)], p1_recv.at[x], at_x(d))
    p1_recv[pl.ds(x, 1)] = p1_send[pl.ds(x, 1)]

    def w_x(c, rows=slice(0, xr)):
        return w_all.at[c, pl.ds(rows.start, rows.stop - rows.start), :]

    def w_y(c, lo=xr, hi=wrows):
        return w_all.at[c, pl.ds(lo, hi - lo), :]

    def bundle(d, lo=0, hi=NX):
        return w_all.at[pl.ds(yp(d) * NX + lo, hi - lo), pl.ds(0, xr), :]

    x_lo, x_hi = slice(0, xr // 32 * 16), slice(xr // 32 * 16, xr)
    y_mid = xr + yr // 32 * 16

    def c_at(dy, dx):
        return yp(dy) * NX + xp(dx)

    def y1_part(step, way, d):
        if step < ry:
            return w_y(c_at(d, 0))
        return w_y(c_at(d, 0), xr, y_mid) if way == 1 else w_y(c_at(d, 0), y_mid)

    def y1_send(step, way):
        part = y1_part(step, way, way * (1 - step))
        net.send(("y1", step, way), part, part, at_y(way))

    def y2_send(d):
        for way in (1, -1):
            net.send(("y2", d, way), w_y(c_at(d, 0)), w_y(c_at(d, 0)), at_x(way))

    def y3_way(d):
        return 1 if 0 <= d < ry else -1

    def x1_send():
        for way in (1, -1):
            net.send(("x1", way), w_x(ctx), w_x(ctx), at_x(way))

    def x2_part(step, way, d):
        if step < ry:
            return bundle(d)
        return bundle(d, 0, NX // 2) if way == 1 else bundle(d, NX // 2, NX)

    def x2_send(step, way):
        part = x2_part(step, way, way * (1 - step))
        net.send(("x2", step, way), part, part, at_y(way))

    seen = set()

    def w_event(event):
        kind, way = event[0], event[-1]
        seen.add(event)
        if kind == "y1":
            step = event[1]
            net.arrive(event, y1_part(step, way, -way * step), at_y(-way))
            if step < ry:
                y1_send(step + 1, way)
        elif kind == "s2":
            y2_send(event[1])
        elif kind == "y2":
            d = event[1]
            part = w_y(c_at(d, -way))
            net.arrive(event, part, at_x(-way))
            if way == y3_way(d):
                net.send(("y3", d), part, part, at_x(way))
        elif kind == "y3":
            d = event[1]
            net.arrive(event, w_y(c_at(d, 2)), at_x(-y3_way(d)))
        elif kind == "x1":
            net.arrive(event, w_x(c_at(0, -way)), at_x(-way))
            part = w_x(c_at(0, -way), x_lo if way == 1 else x_hi)
            net.send(("x1r", way), part, part, at_x(way))
        elif kind == "x1r":
            net.arrive(event, w_x(c_at(0, 2), x_lo if way == 1 else x_hi), at_x(-way))
            if ("x1r", -way) in seen:
                x2_send(1, 1)
                x2_send(1, -1)
        elif kind == "x2":
            step = event[1]
            net.arrive(event, x2_part(step, way, -way * step), at_y(-way))
            if step < ry:
                x2_send(step + 1, way)

    def attend(h):
        lanes = slice(h * hs, (h + 1) * hs)
        for i in range(4):
            rows, upto = slice(i * strip, (i + 1) * strip), (i + 1) * strip
            scores = lax.dot_general(q[rows, lanes], k[0:upto, lanes], NT, preferred_element_type=F32)
            here = col[h, rows, 0:1]
            pieces = []
            for j in range(i + 1):
                gap = here - row[h][:, j * strip : (j + 1) * strip]
                if j == i:
                    gap = jnp.where(t_in >= s_in, gap, -1e30)
                pieces.append((scores[:, j * strip : (j + 1) * strip] * jnp.exp(gap)).astype(BF16))
            weights = jnp.concatenate(pieces, axis=1) if i else pieces[0]
            intra[h, rows, :] = jnp.dot(weights, v[0:upto, lanes], preferred_element_type=F32)

    loads[2].wait()
    x1_send()
    y1_send(1, 1)
    y1_send(1, -1)
    y2_send(0)
    loads[3].wait()
    attend(0)

    for d in range(1, NX):
        net.arrive(("p1", d), p1_recv.at[xp(-d)], at_x(-d))
    inside, before = [], []
    run = [jnp.zeros((quarter, hs), F32) for _ in range(heads)]
    run_decay = [jnp.ones((1, hs), F32) for _ in range(heads)]
    for i in range(NX):
        inside.append(run)
        before.append(run_decay)
        decays = read_decays(p1_recv[i, depth : depth + 16, :])
        states = [p1_recv[i, h * quarter : (h + 1) * quarter, :].astype(F32) for h in range(heads)]
        run = [run[h] * decays[h] + states[h] for h in range(heads)]
        run_decay = [run_decay[h] * decays[h] for h in range(heads)]
    for h in range(heads):
        p2_send[h * quarter : (h + 1) * quarter, :] = run[h].astype(BF16)
    p2_send[depth : depth + 16, :] = decay_rows(run_decay)
    for d in sorted(range(1, ny), key=lambda d: -min(d, ny - d)):
        net.send(("p2", d), p2_send, p2_recv.at[d - 1], at_y(d), when=y + d < ny)

    for event in BEFORE_INCOMING:
        w_event(event)
    attend(1)

    for d in range(1, ny):
        net.arrive(("p2", d), p2_recv.at[d - 1], at_y(-d), when=y >= d)
    rows_before = [jnp.zeros((quarter, hs), F32) for _ in range(heads)]
    for d in range(ny - 1, 0, -1):
        there = y >= d
        decays = read_decays(p2_recv[d - 1, depth : depth + 16, :])
        for h in range(heads):
            state = p2_recv[d - 1, h * quarter : (h + 1) * quarter, :].astype(F32)
            rows_before[h] = jnp.where(there, rows_before[h] * decays[h] + state, 0.0)
    for i in range(NX):
        for h in range(heads):
            p3_send[i, h * quarter : (h + 1) * quarter, :] = (
                rows_before[h] * before[i][h] + inside[i][h]
            ).astype(BF16)
    for d in (2, 1, 3):
        net.send(("p3", d), p3_send.at[xp(d)], p3_recv.at[x], at_x(d))
    p3_recv[pl.ds(x, 1)] = p3_send[pl.ds(x, 1)]
    for event in BEFORE_MIXED:
        w_event(event)

    for d in range(1, NX):
        net.arrive(("p3", d), p3_recv.at[xp(-d)], at_x(-d))

    def piece(t, part):
        return a_all.at[t, pl.ds(part * half, half), :]

    def z_item(i, way):
        return -way * (i // 2), (i % 2 if way == 1 else 1 - i % 2)

    def z_send(i, way):
        d, part = z_item(i, way)
        own = piece(zp(d) * 2 + core, part)
        net.send(("z", i, way), own, own, at_z(way))

    def z_wait(i, way):
        d, part = z_item(i, way)
        net.arrive(("z", i, way), piece(zp(d - way) * 2 + core, part), at_z(-way))

    def hand(d, part):
        own = piece(zp(d) * 2 + core, part)
        net.send(("hand", d, part), own, own, partner)

    def hand_wait(d, part):
        net.arrive(("hand", d, part), piece(zp(d) * 2 + (1 - core), part), partner)

    incoming = [
        jnp.concatenate([p3_recv[i, h * quarter : (h + 1) * quarter, :] for i in range(NX)], axis=0)
        for h in range(heads)
    ]
    loads[7].wait()
    for part in range(2):
        rows = slice(part * half, (part + 1) * half)
        for h in range(heads):
            lanes = slice(h * hs, (h + 1) * hs)
            carried = jnp.dot(q[rows, lanes], incoming[h], preferred_element_type=F32)
            mixed = intra[h, rows, :] + jnp.exp(col[h, rows, :]) * carried
            scale = lax.rsqrt(jnp.mean(mixed * mixed, axis=1, keepdims=True) + EPSILON)
            a_all[ten, rows, lanes] = (mixed * scale * gain_ref[:, lanes]).astype(BF16)
        z_send(part, 1)
        z_send(1 - part, -1) if part else None
    z_send(1, -1)
    hand(0, 0)
    hand(0, 1)

    def multiply(d, part, first=False):
        rows = pl.ds(part * half, half)
        base = zp(d)
        result = None
        for c in range(2):
            weight = w_all[pl.ds(base * 4 + 2 * c, 2)].reshape(2 * wrows, -1)
            term = jnp.dot(a_all[base * 2 + c, rows, :], weight, preferred_element_type=F32)
            result = term if result is None else result + term
        if first:
            acc[rows, :] = result
        else:
            acc[rows, :] += result

    last = 2 * rz - 2

    def z_event(i, way):
        z_wait(i, way)
        if i + 2 <= last:
            z_send(i + 2, way)
        d, part = z_item(i, way)
        hand(d - way, part)

    for event in AFTER_MIXED:
        if event[0] == "z":
            z_event(*event[1:])
        else:
            w_event(event)
    for d in (0, -1, 1, -2, 2):
        for part in range(2):
            hand_wait(d, part)
            multiply(d, part, d == 0)
    z_event(last, 1)
    z_event(last, -1)
    for d in (-3, 3):
        for part in range(2):
            hand_wait(d, part)
            multiply(d, part)
    loads[4].wait()
    for part in range(2):
        rows = pl.ds(part * half, half)
        d = -4 if part == 0 else 4
        hand_wait(d, part)
        multiply(d, part)
        out_ref[0, rows, :] = (res[rows, :].astype(F32) + acc[rows, :]).astype(BF16)
    net.drain()


def local(dims, queries, keys, spike_counts, spike_scale, log_decay, norm_gain, out_weight, residual_in):
    ny, nz, heads, hs, block, wrows, xr = dims
    width = heads * hs
    columns = out_weight.shape[1]
    depth = heads * hs // NX + 16
    vmem = pl.BlockSpec(memory_space=pltpu.VMEM)
    hbm = pl.BlockSpec(memory_space=pltpu.HBM)
    return pl.pallas_call(
        functools.partial(kernel, dims),
        out_shape=pltpu.VMEM((1, block, columns), BF16),
        in_specs=[hbm] * 8,
        out_specs=vmem,
        scratch_shapes=[
            pltpu.VMEM((block, width), BF16),
            pltpu.VMEM((block, width), BF16),
            pltpu.VMEM((block, width), jnp.int32),
            pltpu.VMEM((1, width), F32),
            pltpu.VMEM((1, heads, block), F32),
            pltpu.VMEM((1, width), F32),
            pltpu.VMEM((block, columns), BF16),
            pltpu.VMEM((block, width), BF16),
            pltpu.VMEM((block, columns), F32),
            pltpu.VMEM((heads, block, hs), F32),
            pltpu.VMEM((heads, block, hs), F32),
            pltpu.VMEM((2 * nz, block, width), BF16),
            pltpu.VMEM((ny * NX, wrows, columns), BF16),
            pltpu.VMEM((NX, depth, hs), BF16),
            pltpu.VMEM((NX, depth, hs), BF16),
            pltpu.VMEM((depth, hs), BF16),
            pltpu.VMEM((ny - 1, depth, hs), BF16),
            pltpu.VMEM((NX, depth - 16, hs), BF16),
            pltpu.VMEM((NX, depth - 16, hs), BF16),
            pltpu.SemaphoreType.DMA((96,)),
            pltpu.SemaphoreType.DMA((96,)),
            pltpu.SemaphoreType.DMA((8,)),
        ],
        compiler_params=pltpu.CompilerParams(
            collective_id=0, has_side_effects=True, vmem_limit_bytes=60 * 1024 * 1024
        ),
    )(
        queries, keys, spike_counts, spike_scale.reshape(1, width), log_decay,
        norm_gain.reshape(1, width), out_weight, residual_in,
    )


def solution(mesh):
    ny, nz = mesh.shape["context"] // NX, mesh.shape["tensor"] // 2

    def whole(queries, keys, spike_counts, spike_scale, log_decay, norm_gain, out_weight, residual_in):
        heads = log_decay.shape[1] // (2 * nz)
        hs = queries.shape[2] // log_decay.shape[1]
        block = queries.shape[1] // (ny * NX)
        wrows = out_weight.shape[0] // (ny * NX)
        xr = wrows * 3 // 8
        dims = (ny, nz, heads, hs, block, wrows, xr)
        in_specs = (
            P(None, "context", "tensor"),
            P(None, "context", "tensor"),
            P(None, "context", "tensor"),
            P("tensor"),
            P(None, "tensor", "context"),
            P("tensor"),
            P("context", "tensor"),
            P(None, "context", "tensor"),
        )
        return jax.shard_map(
            functools.partial(local, dims),
            mesh=mesh,
            in_specs=in_specs,
            out_specs=P(None, "context", "tensor"),
            check_vma=False,
        )(queries, keys, spike_counts, spike_scale, log_decay, norm_gain, out_weight, residual_in)

    return whole
```

```python
import functools

import jax
import jax.numpy as jnp
from jax import lax
from jax.experimental import pallas as pl
from jax.experimental.pallas import tpu as pltpu
from jax.sharding import PartitionSpec as P

MESH = pl.DeviceIdType.MESH
NX = 4
EPSILON = 1e-06
F32 = jnp.float32
BF16 = jnp.bfloat16
NT = (((1,), (1,)), ((), ()))
TN = (((0,), (0,)), ((), ()))


BEFORE_INCOMING = (
    ("x1", 1), ("x1", -1), ("y1", 1, 1), ("y1", 1, -1), ("s2", 1), ("s2", -1), ("x1r", 1), ("x1r", -1),
)
BEFORE_MIXED = (
    ("y2", 0, -1), ("y2", 0, 1), ("y1", 2, 1), ("y1", 2, -1), ("y2", 1, 1), ("y2", 1, -1), ("s2", -2), ("s2", 2),
    ("y2", -1, 1), ("y2", -1, -1),
)
AFTER_MIXED = (
    ("y3", 0), ("y2", -2, -1), ("x2", 1, -1), ("x2", 1, 1), ("y3", 1), ("y2", 2, -1), ("y1", 3, -1), ("s2", 3),
    ("y1", 3, 1), ("s2", -3), ("z", 0, -1), ("z", 0, 1), ("y2", -2, 1), ("y3", -1), ("z", 1, -1), ("z", 1, 1),
    ("y2", 2, 1), ("y3", -2), ("z", 2, -1), ("z", 2, 1), ("x2", 2, -1), ("x2", 2, 1), ("y2", 3, 1), ("y1", 4, 1),
    ("y2", 3, -1), ("y1", 4, -1), ("s2", 4), ("z", 3, -1), ("z", 3, 1), ("y2", -3, 1), ("y2", -3, -1), ("z", 4, -1),
    ("z", 4, 1), ("z", 5, -1), ("z", 5, 1), ("y3", 2), ("y2", 4, -1), ("z", 6, -1), ("z", 6, 1), ("y3", 3),
    ("x2", 3, -1), ("x2", 3, 1), ("y3", -3), ("z", 7, -1), ("z", 7, 1), ("y2", 4, 1), ("z", 8, -1), ("z", 8, 1),
    ("y3", 4), ("z", 9, -1), ("z", 9, 1), ("x2", 4, -1), ("x2", 4, 1),
)
AFTER_WEIGHTS = (
    ("z", 10, -1), ("z", 10, 1), ("z", 11, -1), ("z", 11, 1), ("z", 12, -1), ("z", 12, 1), ("z", 13, -1),
    ("z", 13, 1),
)


class Net:
    def __init__(self, send_sem, recv_sem):
        self.send_sem, self.recv_sem = send_sem, recv_sem
        self.number = {}
        self.sent = []

    def slot(self, name):
        return self.number.setdefault(name, len(self.number))

    def copy(self, name, src, dst, target):
        i = self.slot(name)
        return pltpu.make_async_remote_copy(
            src_ref=src,
            dst_ref=dst,
            send_sem=self.send_sem.at[i],
            recv_sem=self.recv_sem.at[i],
            device_id=target,
            device_id_type=MESH,
        )

    def send(self, name, src, dst, target, when=None):
        copy = self.copy(name, src, dst, target)
        if when is None:
            copy.start()
        else:
            pl.when(when)(copy.start)
        self.sent.append((copy, when))

    def arrive(self, name, place, source, when=None):
        copy = self.copy(name, place, place, source)
        if when is None:
            copy.wait_recv()
        else:
            pl.when(when)(copy.wait_recv)

    def drain(self):
        for copy, when in self.sent:
            if when is None:
                copy.wait_send()
            else:
                pl.when(when)(copy.wait_send)


def kernel(
    dims,
    q_hbm, k_hbm, cnt_hbm, scale_hbm, ld_hbm, gain_hbm, w_hbm, res_hbm, out_ref,
    q, k, cnt, scale_ref, ld_ref, gain_ref, res, v, acc, col, intra, a_all, w_all,
    p1_send, p1_recv, p2_send, p2_recv, p3_send, p3_recv,
    send_sem, recv_sem, load_sem,
):
    ny, nz, heads, hs, block, wrows, xr = dims
    ctx, ten = lax.axis_index("context"), lax.axis_index("tensor")
    y, x = ctx // NX, ctx % NX
    z, core = ten // 2, ten % 2
    quarter = hs // NX
    half = block // 2
    ry, rz = ny // 2, nz // 2
    yr = wrows - xr
    span = 2 * heads * hs // wrows

    def yp(d):
        return lax.rem(y + (d + ny), ny)

    def xp(d):
        return lax.rem(x + (d + NX), NX)

    def zp(d):
        return lax.rem(z + (d + nz), nz)

    def at_y(d):
        return (yp(d) * NX + x, ten)

    def at_x(d):
        return (y * NX + xp(d), ten)

    def at_z(d):
        return (ctx, zp(d) * 2 + core)

    partner = (ctx, z * 2 + (1 - core))
    net = Net(send_sem, recv_sem)

    loads = [
        pltpu.make_async_copy(k_hbm.at[0], k, load_sem.at[0]),
        pltpu.make_async_copy(cnt_hbm.at[0], cnt, load_sem.at[1]),
        pltpu.make_async_copy(w_hbm, w_all.at[ctx], load_sem.at[2]),
        pltpu.make_async_copy(q_hbm.at[0], q, load_sem.at[3]),
        pltpu.make_async_copy(res_hbm.at[0], res, load_sem.at[4]),
        pltpu.make_async_copy(ld_hbm, ld_ref, load_sem.at[5]),
        pltpu.make_async_copy(scale_hbm, scale_ref, load_sem.at[6]),
        pltpu.make_async_copy(gain_hbm, gain_ref, load_sem.at[7]),
    ]
    for i in (5, 6, 0, 1, 2, 3, 7, 4):
        loads[i].start()
    barrier = pltpu.get_barrier_semaphore()
    friends = [at_y(d) for d in range(1, ny)] + [at_x(d) for d in range(1, NX)]
    friends += [at_z(1), at_z(-1), partner]
    for friend in friends:
        pl.semaphore_signal(barrier, inc=1, device_id=friend, device_id_type=MESH)

    strip = block // 4
    t_in = lax.broadcasted_iota(jnp.int32, (strip, strip), 0)
    s_in = lax.broadcasted_iota(jnp.int32, (strip, strip), 1)
    tri = jnp.where(t_in >= s_in, 1.0, 0.0).astype(BF16)

    def parts(value):
        hi = value.astype(BF16)
        rest = value - hi.astype(F32)
        mid = rest.astype(BF16)
        return hi, mid, (rest - mid.astype(F32)).astype(BF16)

    loads[5].wait()
    row = []
    for h in range(heads):
        base, pieces = None, []
        for i in range(4):
            rates = ld_ref[0, h : h + 1, i * strip : (i + 1) * strip]
            down = along = None
            for part in parts(jnp.broadcast_to(rates, (hs, strip))):
                term = lax.dot_general(tri, part, NT, preferred_element_type=F32)
                down = term if down is None else down + term
                term = lax.dot_general(part[0:16], tri, NT, preferred_element_type=F32)
                along = term if along is None else along + term
            if i:
                down, along = down + base, along + base
            col[h, i * strip : (i + 1) * strip, :] = down
            base = down[strip - 1 : strip, :]
            pieces.append(along[0:1, :])
        row.append(jnp.concatenate(pieces, axis=1))

    loads[0].wait()
    loads[1].wait()
    loads[6].wait()
    v[...] = (cnt[...].astype(F32) * scale_ref[...]).astype(BF16)

    def decay_rows(decays):
        index = lax.broadcasted_iota(jnp.int32, (16, hs), 0)
        rows = jnp.zeros((16, hs), F32)
        for h, decay in enumerate(decays):
            hi = decay.astype(BF16).astype(F32)
            rows = jnp.where(index == 2 * h, hi, rows)
            rows = jnp.where(index == 2 * h + 1, decay - hi, rows)
        return rows.astype(BF16)

    def read_decays(tile):
        rows = tile.astype(F32)
        return [rows[2 * h : 2 * h + 1, :] + rows[2 * h + 1 : 2 * h + 2, :] for h in range(heads)]

    depth = heads * quarter
    own_decay = []
    for h in range(heads):
        lanes = slice(h * hs, (h + 1) * hs)
        last = col[h, block - 1 : block, :]
        to_end = jnp.exp(last - col[h])
        weighted = (k[:, lanes].astype(F32) * to_end).astype(BF16)
        state = lax.dot_general(weighted, v[:, lanes], TN, preferred_element_type=F32)
        for part in range(NX):
            p1_send[part, h * quarter : (h + 1) * quarter, :] = state[
                part * quarter : (part + 1) * quarter, :
            ].astype(BF16)
        own_decay.append(jnp.exp(last))
    own_rows = decay_rows(own_decay)
    for part in range(NX):
        p1_send[part, depth : depth + 16, :] = own_rows

    pl.semaphore_wait(barrier, len(friends))

    for d in (2, 1, 3):
        net.send(("p1", d), p1_send.at[xp(d)], p1_recv.at[x], at_x(d))
    p1_recv[pl.ds(x, 1)] = p1_send[pl.ds(x, 1)]

    def w_x(c, rows=slice(0, xr)):
        return w_all.at[c, pl.ds(rows.start, rows.stop - rows.start), :]

    def w_y(c, lo=xr, hi=wrows):
        return w_all.at[c, pl.ds(lo, hi - lo), :]

    def bundle(d, lo=0, hi=NX):
        return w_all.at[pl.ds(yp(d) * NX + lo, hi - lo), pl.ds(0, xr), :]

    x_lo, x_hi = slice(0, xr // 32 * 16), slice(xr // 32 * 16, xr)
    y_mid = xr + yr // 32 * 16

    def c_at(dy, dx):
        return yp(dy) * NX + xp(dx)

    def y1_part(step, way, d):
        if step < ry:
            return w_y(c_at(d, 0))
        return w_y(c_at(d, 0), xr, y_mid) if way == 1 else w_y(c_at(d, 0), y_mid)

    def y1_send(step, way):
        part = y1_part(step, way, way * (1 - step))
        net.send(("y1", step, way), part, part, at_y(way))

    def y2_send(d):
        for way in (1, -1):
            net.send(("y2", d, way), w_y(c_at(d, 0)), w_y(c_at(d, 0)), at_x(way))

    def y3_way(d):
        return 1 if 0 <= d < ry else -1

    def x1_send():
        for way in (1, -1):
            net.send(("x1", way), w_x(ctx), w_x(ctx), at_x(way))

    def x2_part(step, way, d):
        if step < ry:
            return bundle(d)
        return bundle(d, 0, NX // 2) if way == 1 else bundle(d, NX // 2, NX)

    def x2_send(step, way):
        part = x2_part(step, way, way * (1 - step))
        net.send(("x2", step, way), part, part, at_y(way))

    seen = set()

    def w_event(event):
        kind, way = event[0], event[-1]
        seen.add(event)
        if kind == "y1":
            step = event[1]
            net.arrive(event, y1_part(step, way, -way * step), at_y(-way))
            if step < ry:
                y1_send(step + 1, way)
        elif kind == "s2":
            y2_send(event[1])
        elif kind == "y2":
            d = event[1]
            part = w_y(c_at(d, -way))
            net.arrive(event, part, at_x(-way))
            if way == y3_way(d):
                net.send(("y3", d), part, part, at_x(way))
        elif kind == "y3":
            d = event[1]
            net.arrive(event, w_y(c_at(d, 2)), at_x(-y3_way(d)))
        elif kind == "x1":
            net.arrive(event, w_x(c_at(0, -way)), at_x(-way))
            part = w_x(c_at(0, -way), x_lo if way == 1 else x_hi)
            net.send(("x1r", way), part, part, at_x(way))
        elif kind == "x1r":
            net.arrive(event, w_x(c_at(0, 2), x_lo if way == 1 else x_hi), at_x(-way))
            if ("x1r", -way) in seen:
                x2_send(1, 1)
                x2_send(1, -1)
        elif kind == "x2":
            step = event[1]
            net.arrive(event, x2_part(step, way, -way * step), at_y(-way))
            if step < ry:
                x2_send(step + 1, way)

    def attend(h):
        lanes = slice(h * hs, (h + 1) * hs)
        for i in range(4):
            rows, upto = slice(i * strip, (i + 1) * strip), (i + 1) * strip
            scores = lax.dot_general(q[rows, lanes], k[0:upto, lanes], NT, preferred_element_type=F32)
            here = col[h, rows, 0:1]
            pieces = []
            for j in range(i + 1):
                gap = here - row[h][:, j * strip : (j + 1) * strip]
                if j == i:
                    gap = jnp.where(t_in >= s_in, gap, -1e30)
                pieces.append((scores[:, j * strip : (j + 1) * strip] * jnp.exp(gap)).astype(BF16))
            weights = jnp.concatenate(pieces, axis=1) if i else pieces[0]
            intra[h, rows, :] = jnp.dot(weights, v[0:upto, lanes], preferred_element_type=F32)

    loads[2].wait()
    x1_send()
    y1_send(1, 1)
    y1_send(1, -1)
    y2_send(0)
    loads[3].wait()
    attend(0)
    attend(1)

    for d in range(1, NX):
        net.arrive(("p1", d), p1_recv.at[xp(-d)], at_x(-d))
    inside, before = [], []
    run = [jnp.zeros((quarter, hs), F32) for _ in range(heads)]
    run_decay = [jnp.ones((1, hs), F32) for _ in range(heads)]
    for i in range(NX):
        inside.append(run)
        before.append(run_decay)
        decays = read_decays(p1_recv[i, depth : depth + 16, :])
        states = [p1_recv[i, h * quarter : (h + 1) * quarter, :].astype(F32) for h in range(heads)]
        run = [run[h] * decays[h] + states[h] for h in range(heads)]
        run_decay = [run_decay[h] * decays[h] for h in range(heads)]
    for h in range(heads):
        p2_send[h * quarter : (h + 1) * quarter, :] = run[h].astype(BF16)
    p2_send[depth : depth + 16, :] = decay_rows(run_decay)
    for d in sorted(range(1, ny), key=lambda d: -min(d, ny - d)):
        net.send(("p2", d), p2_send, p2_recv.at[d - 1], at_y(d), when=y + d < ny)

    for event in BEFORE_INCOMING:
        w_event(event)

    for d in range(1, ny):
        net.arrive(("p2", d), p2_recv.at[d - 1], at_y(-d), when=y >= d)
    rows_before = [jnp.zeros((quarter, hs), F32) for _ in range(heads)]
    for d in range(ny - 1, 0, -1):
        there = y >= d
        decays = read_decays(p2_recv[d - 1, depth : depth + 16, :])
        for h in range(heads):
            state = p2_recv[d - 1, h * quarter : (h + 1) * quarter, :].astype(F32)
            rows_before[h] = jnp.where(there, rows_before[h] * decays[h] + state, 0.0)
    for i in range(NX):
        for h in range(heads):
            p3_send[i, h * quarter : (h + 1) * quarter, :] = (
                rows_before[h] * before[i][h] + inside[i][h]
            ).astype(BF16)
    for d in (2, 1, 3):
        net.send(("p3", d), p3_send.at[xp(d)], p3_recv.at[x], at_x(d))
    p3_recv[pl.ds(x, 1)] = p3_send[pl.ds(x, 1)]
    for event in BEFORE_MIXED:
        w_event(event)

    for d in range(1, NX):
        net.arrive(("p3", d), p3_recv.at[xp(-d)], at_x(-d))

    def piece(t, part):
        return a_all.at[t, pl.ds(part * strip, strip), :]

    def z_item(i, way):
        return -way * (i // 4), (i % 4 if way == 1 else (i + 2) % 4)

    def z_send(i, way):
        d, part = z_item(i, way)
        own = piece(zp(d) * 2 + core, part)
        net.send(("z", i, way), own, own, at_z(way))

    def z_wait(i, way):
        d, part = z_item(i, way)
        net.arrive(("z", i, way), piece(zp(d - way) * 2 + core, part), at_z(-way))

    def hand(d, part):
        own = piece(zp(d) * 2 + core, part)
        net.send(("hand", d, part), own, own, partner)

    def hand_wait(d, part):
        net.arrive(("hand", d, part), piece(zp(d) * 2 + (1 - core), part), partner)

    incoming = [
        jnp.concatenate([p3_recv[i, h * quarter : (h + 1) * quarter, :] for i in range(NX)], axis=0)
        for h in range(heads)
    ]
    loads[7].wait()
    for way, part in ((1, 0), (-1, 2), (1, 1), (-1, 3)):
        rows = slice(part * strip, (part + 1) * strip)
        for h in range(heads):
            lanes = slice(h * hs, (h + 1) * hs)
            carried = jnp.dot(q[rows, lanes], incoming[h], preferred_element_type=F32)
            mixed = intra[h, rows, :] + jnp.exp(col[h, rows, :]) * carried
            scale = lax.rsqrt(jnp.mean(mixed * mixed, axis=1, keepdims=True) + EPSILON)
            a_all[ten, rows, lanes] = (mixed * scale * gain_ref[:, lanes]).astype(BF16)
        z_send(part % 2, way)
    for i in (2, 3):
        z_send(i, 1)
        z_send(i, -1)
    for part in range(4):
        hand(0, part)

    def multiply(d, part):
        rows = pl.ds(part * half, half)
        for i in (2 * part, 2 * part + 1):
            hand_wait(d, i)
        base = zp(d)
        result = None
        for c in range(2):
            weight = w_all[pl.ds(base * span + c * (span // 2), span // 2)].reshape(span // 2 * wrows, -1)
            term = jnp.dot(a_all[base * 2 + c, rows, :], weight, preferred_element_type=F32)
            result = term if result is None else result + term
        return result

    def z_event(i, way):
        z_wait(i, way)
        if i + 4 < 4 * rz - 2:
            z_send(i + 4, way)
        d, part = z_item(i, way)
        hand(d - way, part)

    def run(events):
        for event in events:
            if event[0] == "z":
                z_event(*event[1:])
            else:
                w_event(event)

    run(AFTER_MIXED)
    halves = [pl.ds(part * half, half) for part in range(2)]
    for d in (0, -1, 1, -2, 2):
        for part in range(2):
            if d:
                acc[halves[part], :] += multiply(d, part)
            else:
                acc[halves[part], :] = multiply(d, part)
    run(AFTER_WEIGHTS)
    for d in (-3, 3):
        for part in range(2):
            acc[halves[part], :] += multiply(d, part)
    loads[4].wait()
    for part, d in ((0, -rz), (1, rz)):
        total = acc[halves[part], :] + multiply(d, part)
        out_ref[0, halves[part], :] = (res[halves[part], :].astype(F32) + total).astype(BF16)
    net.drain()


def local(dims, queries, keys, spike_counts, spike_scale, log_decay, norm_gain, out_weight, residual_in):
    ny, nz, heads, hs, block, wrows, xr = dims
    width = heads * hs
    columns = out_weight.shape[1]
    depth = heads * hs // NX + 16
    vmem = pl.BlockSpec(memory_space=pltpu.VMEM)
    hbm = pl.BlockSpec(memory_space=pltpu.HBM)
    return pl.pallas_call(
        functools.partial(kernel, dims),
        out_shape=pltpu.VMEM((1, block, columns), BF16),
        in_specs=[hbm] * 8,
        out_specs=vmem,
        scratch_shapes=[
            pltpu.VMEM((block, width), BF16),
            pltpu.VMEM((block, width), BF16),
            pltpu.VMEM((block, width), jnp.int32),
            pltpu.VMEM((1, width), F32),
            pltpu.VMEM((1, heads, block), F32),
            pltpu.VMEM((1, width), F32),
            pltpu.VMEM((block, columns), BF16),
            pltpu.VMEM((block, width), BF16),
            pltpu.VMEM((block, columns), F32),
            pltpu.VMEM((heads, block, hs), F32),
            pltpu.VMEM((heads, block, hs), F32),
            pltpu.VMEM((2 * nz, block, width), BF16),
            pltpu.VMEM((ny * NX, wrows, columns), BF16),
            pltpu.VMEM((NX, depth, hs), BF16),
            pltpu.VMEM((NX, depth, hs), BF16),
            pltpu.VMEM((depth, hs), BF16),
            pltpu.VMEM((ny - 1, depth, hs), BF16),
            pltpu.VMEM((NX, depth - 16, hs), BF16),
            pltpu.VMEM((NX, depth - 16, hs), BF16),
            pltpu.SemaphoreType.DMA((120,)),
            pltpu.SemaphoreType.DMA((120,)),
            pltpu.SemaphoreType.DMA((8,)),
        ],
        compiler_params=pltpu.CompilerParams(
            collective_id=0, has_side_effects=True, vmem_limit_bytes=60 * 1024 * 1024
        ),
    )(
        queries, keys, spike_counts, spike_scale.reshape(1, width), log_decay,
        norm_gain.reshape(1, width), out_weight, residual_in,
    )


def solution(mesh):
    ny, nz = mesh.shape["context"] // NX, mesh.shape["tensor"] // 2

    def whole(queries, keys, spike_counts, spike_scale, log_decay, norm_gain, out_weight, residual_in):
        heads = log_decay.shape[1] // (2 * nz)
        hs = queries.shape[2] // log_decay.shape[1]
        block = queries.shape[1] // (ny * NX)
        wrows = out_weight.shape[0] // (ny * NX)
        xr = wrows * 3 // 8
        dims = (ny, nz, heads, hs, block, wrows, xr)
        in_specs = (
            P(None, "context", "tensor"),
            P(None, "context", "tensor"),
            P(None, "context", "tensor"),
            P("tensor"),
            P(None, "tensor", "context"),
            P("tensor"),
            P("context", "tensor"),
            P(None, "context", "tensor"),
        )
        return jax.shard_map(
            functools.partial(local, dims),
            mesh=mesh,
            in_specs=in_specs,
            out_specs=P(None, "context", "tensor"),
            check_vma=False,
        )(queries, keys, spike_counts, spike_scale, log_decay, norm_gain, out_weight, residual_in)

    return whole
```

```python
import functools

import jax
import jax.numpy as jnp
from jax import lax
from jax.experimental import pallas as pl
from jax.experimental.pallas import tpu as pltpu
from jax.sharding import PartitionSpec as P

MESH = pl.DeviceIdType.MESH
NX = 4
EPSILON = 1e-06
F32 = jnp.float32
BF16 = jnp.bfloat16
NT = (((1,), (1,)), ((), ()))
TN = (((0,), (0,)), ((), ()))


BEFORE_INCOMING = (
    ("x1", 1), ("x1", -1), ("y1", 1, 1), ("y1", 1, -1), ("s2", 1), ("s2", -1), ("x1r", 1), ("x1r", -1),
)
BEFORE_MIXED = (
    ("y2", 0, -1), ("y2", 0, 1), ("y1", 2, 1), ("y1", 2, -1), ("y2", 1, 1), ("s2", -2), ("s2", 2), ("y2", 1, -1),
    ("y2", -1, 1), ("y2", -1, -1),
)
AFTER_MIXED = (
    ("y3", 0), ("y2", -2, -1), ("x2", 1, -1), ("x2", 1, 1), ("y3", 1), ("y2", 2, -1), ("y1", 3, -1), ("s2", 3),
    ("y1", 3, 1), ("s2", -3), ("y2", -2, 1), ("z", 0, -1), ("z", 0, 1), ("y3", -1), ("z", 1, -1), ("z", 1, 1),
    ("y2", 2, 1), ("y3", -2), ("z", 2, -1), ("z", 2, 1), ("x2", 2, -1), ("x2", 2, 1), ("y2", 3, 1), ("y2", 3, -1),
    ("y1", 4, 1), ("z", 3, -1), ("z", 3, 1), ("y1", 4, -1), ("s2", 4), ("y2", -3, 1), ("y2", -3, -1), ("z", 4, -1),
    ("z", 4, 1), ("y3", 2), ("z", 5, -1), ("z", 5, 1), ("y2", 4, -1), ("z", 6, -1), ("z", 6, 1), ("y3", 3),
    ("x2", 3, -1), ("x2", 3, 1), ("z", 7, -1), ("z", 7, 1), ("y3", -3), ("y2", 4, 1), ("z", 8, -1), ("z", 8, 1),
    ("y3", 4), ("z", 9, -1), ("z", 9, 1), ("x2", 4, -1), ("x2", 4, 1),
)
AFTER_WEIGHTS = (
    ("z", 10, -1), ("z", 10, 1), ("z", 11, -1), ("z", 11, 1), ("z", 12, -1), ("z", 12, 1), ("z", 13, -1),
    ("z", 13, 1),
)


class Net:
    def __init__(self, send_sem, recv_sem):
        self.send_sem, self.recv_sem = send_sem, recv_sem
        self.number = {}
        self.sent = []

    def slot(self, name):
        return self.number.setdefault(name, len(self.number))

    def copy(self, name, src, dst, target):
        i = self.slot(name)
        return pltpu.make_async_remote_copy(
            src_ref=src,
            dst_ref=dst,
            send_sem=self.send_sem.at[i],
            recv_sem=self.recv_sem.at[i],
            device_id=target,
            device_id_type=MESH,
        )

    def send(self, name, src, dst, target, when=None):
        copy = self.copy(name, src, dst, target)
        if when is None:
            copy.start()
        else:
            pl.when(when)(copy.start)
        self.sent.append((copy, when))

    def arrive(self, name, place, source, when=None):
        copy = self.copy(name, place, place, source)
        if when is None:
            copy.wait_recv()
        else:
            pl.when(when)(copy.wait_recv)

    def drain(self):
        for copy, when in self.sent:
            if when is None:
                copy.wait_send()
            else:
                pl.when(when)(copy.wait_send)


def kernel(
    dims,
    q_hbm, k_hbm, cnt_hbm, scale_hbm, ld_hbm, gain_hbm, w_hbm, res_hbm, out_ref,
    q, k, cnt, scale_ref, ld_ref, gain_ref, res, v, acc, col, intra, a_all, w_all,
    p1_send, p1_recv, p2_send, p2_recv, p3_send, p3_recv,
    send_sem, recv_sem, load_sem,
):
    ny, nz, heads, hs, block, wrows, xr = dims
    ctx, ten = lax.axis_index("context"), lax.axis_index("tensor")
    y, x = ctx // NX, ctx % NX
    z, core = ten // 2, ten % 2
    quarter = hs // NX
    half = block // 2
    ry, rz = ny // 2, nz // 2
    yr = wrows - xr
    span = 2 * heads * hs // wrows

    def yp(d):
        return lax.rem(y + (d + ny), ny)

    def xp(d):
        return lax.rem(x + (d + NX), NX)

    def zp(d):
        return lax.rem(z + (d + nz), nz)

    def at_y(d):
        return (yp(d) * NX + x, ten)

    def at_x(d):
        return (y * NX + xp(d), ten)

    def at_z(d):
        return (ctx, zp(d) * 2 + core)

    partner = (ctx, z * 2 + (1 - core))
    net = Net(send_sem, recv_sem)

    loads = [
        pltpu.make_async_copy(k_hbm.at[0], k, load_sem.at[0]),
        pltpu.make_async_copy(cnt_hbm.at[0], cnt, load_sem.at[1]),
        pltpu.make_async_copy(w_hbm, w_all.at[ctx], load_sem.at[2]),
        pltpu.make_async_copy(q_hbm.at[0], q, load_sem.at[3]),
        pltpu.make_async_copy(res_hbm.at[0], res, load_sem.at[4]),
        pltpu.make_async_copy(ld_hbm, ld_ref, load_sem.at[5]),
        pltpu.make_async_copy(scale_hbm, scale_ref, load_sem.at[6]),
        pltpu.make_async_copy(gain_hbm, gain_ref, load_sem.at[7]),
    ]
    for i in (5, 6, 0, 1, 2, 3, 7, 4):
        loads[i].start()
    barrier = pltpu.get_barrier_semaphore()
    friends = [at_y(d) for d in range(1, ny)] + [at_x(d) for d in range(1, NX)]
    friends += [at_z(1), at_z(-1), partner]
    for friend in friends:
        pl.semaphore_signal(barrier, inc=1, device_id=friend, device_id_type=MESH)

    strip = block // 4
    t_in = lax.broadcasted_iota(jnp.int32, (strip, strip), 0)
    s_in = lax.broadcasted_iota(jnp.int32, (strip, strip), 1)
    tri = jnp.where(t_in >= s_in, 1.0, 0.0).astype(BF16)

    def parts(value):
        hi = value.astype(BF16)
        rest = value - hi.astype(F32)
        mid = rest.astype(BF16)
        return hi, mid, (rest - mid.astype(F32)).astype(BF16)

    loads[5].wait()
    row = []
    for h in range(heads):
        base, pieces = None, []
        for i in range(4):
            rates = ld_ref[0, h : h + 1, i * strip : (i + 1) * strip]
            down = along = None
            for part in parts(jnp.broadcast_to(rates, (hs, strip))):
                term = lax.dot_general(tri, part, NT, preferred_element_type=F32)
                down = term if down is None else down + term
                term = lax.dot_general(part[0:16], tri, NT, preferred_element_type=F32)
                along = term if along is None else along + term
            if i:
                down, along = down + base, along + base
            col[h, i * strip : (i + 1) * strip, :] = down
            base = down[strip - 1 : strip, :]
            pieces.append(along[0:1, :])
        row.append(jnp.concatenate(pieces, axis=1))

    loads[0].wait()
    loads[1].wait()
    loads[6].wait()
    v[...] = (cnt[...].astype(F32) * scale_ref[...]).astype(BF16)

    def decay_rows(decays):
        index = lax.broadcasted_iota(jnp.int32, (16, hs), 0)
        rows = jnp.zeros((16, hs), F32)
        for h, decay in enumerate(decays):
            hi = decay.astype(BF16).astype(F32)
            rows = jnp.where(index == 2 * h, hi, rows)
            rows = jnp.where(index == 2 * h + 1, decay - hi, rows)
        return rows.astype(BF16)

    def read_decays(tile):
        rows = tile.astype(F32)
        return [rows[2 * h : 2 * h + 1, :] + rows[2 * h + 1 : 2 * h + 2, :] for h in range(heads)]

    depth = heads * quarter
    own_decay = []
    for h in range(heads):
        lanes = slice(h * hs, (h + 1) * hs)
        last = col[h, block - 1 : block, :]
        to_end = jnp.exp(last - col[h])
        weighted = (k[:, lanes].astype(F32) * to_end).astype(BF16)
        state = lax.dot_general(weighted, v[:, lanes], TN, preferred_element_type=F32)
        for part in range(NX):
            p1_send[part, h * quarter : (h + 1) * quarter, :] = state[
                part * quarter : (part + 1) * quarter, :
            ].astype(BF16)
        own_decay.append(jnp.exp(last))
    own_rows = decay_rows(own_decay)
    for part in range(NX):
        p1_send[part, depth : depth + 16, :] = own_rows

    pl.semaphore_wait(barrier, len(friends))

    for d in (2, 1, 3):
        net.send(("p1", d), p1_send.at[xp(d)], p1_recv.at[x], at_x(d))
    p1_recv[pl.ds(x, 1)] = p1_send[pl.ds(x, 1)]

    def w_x(c, rows=slice(0, xr)):
        return w_all.at[c, pl.ds(rows.start, rows.stop - rows.start), :]

    def w_y(c, lo=xr, hi=wrows):
        return w_all.at[c, pl.ds(lo, hi - lo), :]

    def bundle(d, lo=0, hi=NX):
        return w_all.at[pl.ds(yp(d) * NX + lo, hi - lo), pl.ds(0, xr), :]

    x_lo, x_hi = slice(0, xr // 32 * 16), slice(xr // 32 * 16, xr)
    y_mid = xr + yr // 32 * 16

    def c_at(dy, dx):
        return yp(dy) * NX + xp(dx)

    def y1_part(step, way, d):
        if step < ry:
            return w_y(c_at(d, 0))
        return w_y(c_at(d, 0), xr, y_mid) if way == 1 else w_y(c_at(d, 0), y_mid)

    def y1_send(step, way):
        part = y1_part(step, way, way * (1 - step))
        net.send(("y1", step, way), part, part, at_y(way))

    def y2_send(d):
        for way in (1, -1):
            net.send(("y2", d, way), w_y(c_at(d, 0)), w_y(c_at(d, 0)), at_x(way))

    def y3_way(d):
        return 1 if 0 <= d < ry else -1

    def x1_send():
        for way in (1, -1):
            net.send(("x1", way), w_x(ctx), w_x(ctx), at_x(way))

    def x2_part(step, way, d):
        if step < ry:
            return bundle(d)
        return bundle(d, 0, NX // 2) if way == 1 else bundle(d, NX // 2, NX)

    def x2_send(step, way):
        part = x2_part(step, way, way * (1 - step))
        net.send(("x2", step, way), part, part, at_y(way))

    seen = set()

    def w_event(event):
        kind, way = event[0], event[-1]
        seen.add(event)
        if kind == "y1":
            step = event[1]
            net.arrive(event, y1_part(step, way, -way * step), at_y(-way))
            if step < ry:
                y1_send(step + 1, way)
        elif kind == "s2":
            y2_send(event[1])
        elif kind == "y2":
            d = event[1]
            part = w_y(c_at(d, -way))
            net.arrive(event, part, at_x(-way))
            if way == y3_way(d):
                net.send(("y3", d), part, part, at_x(way))
        elif kind == "y3":
            d = event[1]
            net.arrive(event, w_y(c_at(d, 2)), at_x(-y3_way(d)))
        elif kind == "x1":
            net.arrive(event, w_x(c_at(0, -way)), at_x(-way))
            part = w_x(c_at(0, -way), x_lo if way == 1 else x_hi)
            net.send(("x1r", way), part, part, at_x(way))
        elif kind == "x1r":
            net.arrive(event, w_x(c_at(0, 2), x_lo if way == 1 else x_hi), at_x(-way))
            if ("x1r", -way) in seen:
                x2_send(1, 1)
                x2_send(1, -1)
        elif kind == "x2":
            step = event[1]
            net.arrive(event, x2_part(step, way, -way * step), at_y(-way))
            if step < ry:
                x2_send(step + 1, way)

    def attend(h):
        lanes = slice(h * hs, (h + 1) * hs)
        for i in range(4):
            rows, upto = slice(i * strip, (i + 1) * strip), (i + 1) * strip
            scores = lax.dot_general(q[rows, lanes], k[0:upto, lanes], NT, preferred_element_type=F32)
            here = col[h, rows, 0:1]
            pieces = []
            for j in range(i + 1):
                gap = here - row[h][:, j * strip : (j + 1) * strip]
                if j == i:
                    gap = jnp.where(t_in >= s_in, gap, -1e30)
                pieces.append((scores[:, j * strip : (j + 1) * strip] * jnp.exp(gap)).astype(BF16))
            weights = jnp.concatenate(pieces, axis=1) if i else pieces[0]
            intra[h, rows, :] = jnp.dot(weights, v[0:upto, lanes], preferred_element_type=F32)

    loads[2].wait()
    x1_send()
    y1_send(1, 1)
    y1_send(1, -1)
    y2_send(0)
    loads[3].wait()
    attend(0)
    attend(1)
    for h in range(heads):
        col[h] = jnp.exp(col[h])

    for d in range(1, NX):
        net.arrive(("p1", d), p1_recv.at[xp(-d)], at_x(-d))
    inside, before = [], []
    run = [jnp.zeros((quarter, hs), F32) for _ in range(heads)]
    run_decay = [jnp.ones((1, hs), F32) for _ in range(heads)]
    for i in range(NX):
        inside.append(run)
        before.append(run_decay)
        decays = read_decays(p1_recv[i, depth : depth + 16, :])
        states = [p1_recv[i, h * quarter : (h + 1) * quarter, :].astype(F32) for h in range(heads)]
        run = [run[h] * decays[h] + states[h] for h in range(heads)]
        run_decay = [run_decay[h] * decays[h] for h in range(heads)]
    for h in range(heads):
        p2_send[h * quarter : (h + 1) * quarter, :] = run[h].astype(BF16)
    p2_send[depth : depth + 16, :] = decay_rows(run_decay)
    for d in sorted(range(1, ny), key=lambda d: -min(d, ny - d)):
        net.send(("p2", d), p2_send, p2_recv.at[d - 1], at_y(d), when=y + d < ny)

    for event in BEFORE_INCOMING:
        w_event(event)

    for d in range(1, ny):
        net.arrive(("p2", d), p2_recv.at[d - 1], at_y(-d), when=y >= d)
    rows_before = [jnp.zeros((quarter, hs), F32) for _ in range(heads)]
    for d in range(ny - 1, 0, -1):
        there = y >= d
        decays = read_decays(p2_recv[d - 1, depth : depth + 16, :])
        for h in range(heads):
            state = p2_recv[d - 1, h * quarter : (h + 1) * quarter, :].astype(F32)
            rows_before[h] = jnp.where(there, rows_before[h] * decays[h] + state, 0.0)
    for i in range(NX):
        for h in range(heads):
            p3_send[i, h * quarter : (h + 1) * quarter, :] = (
                rows_before[h] * before[i][h] + inside[i][h]
            ).astype(BF16)
    for d in (2, 1, 3):
        net.send(("p3", d), p3_send.at[xp(d)], p3_recv.at[x], at_x(d))
    p3_recv[pl.ds(x, 1)] = p3_send[pl.ds(x, 1)]
    for event in BEFORE_MIXED:
        w_event(event)

    for d in range(1, NX):
        net.arrive(("p3", d), p3_recv.at[xp(-d)], at_x(-d))

    def piece(t, part):
        return a_all.at[t, pl.ds(part * strip, strip), :]

    def z_item(i, way):
        return -way * (i // 4), (i % 4 if way == 1 else (i + 2) % 4)

    def z_send(i, way):
        d, part = z_item(i, way)
        own = piece(zp(d) * 2 + core, part)
        net.send(("z", i, way), own, own, at_z(way))

    def z_wait(i, way):
        d, part = z_item(i, way)
        net.arrive(("z", i, way), piece(zp(d - way) * 2 + core, part), at_z(-way))

    def hand(d, part):
        own = piece(zp(d) * 2 + core, part)
        net.send(("hand", d, part), own, own, partner)

    def hand_wait(d, part):
        net.arrive(("hand", d, part), piece(zp(d) * 2 + (1 - core), part), partner)

    incoming = [
        jnp.concatenate([p3_recv[i, h * quarter : (h + 1) * quarter, :] for i in range(NX)], axis=0)
        for h in range(heads)
    ]
    loads[7].wait()
    for way, part in ((1, 0), (-1, 2), (1, 1), (-1, 3)):
        rows = slice(part * strip, (part + 1) * strip)
        for h in range(heads):
            lanes = slice(h * hs, (h + 1) * hs)
            carried = jnp.dot(q[rows, lanes], incoming[h], preferred_element_type=F32)
            mixed = intra[h, rows, :] + col[h, rows, :] * carried
            scale = lax.rsqrt(jnp.mean(mixed * mixed, axis=1, keepdims=True) + EPSILON)
            a_all[ten, rows, lanes] = (mixed * scale * gain_ref[:, lanes]).astype(BF16)
        z_send(part % 2, way)
    for i in (2, 3):
        z_send(i, 1)
        z_send(i, -1)
    for part in range(4):
        hand(0, part)

    def multiply(d, part):
        rows = pl.ds(part * half, half)
        for i in (2 * part, 2 * part + 1):
            hand_wait(d, i)
        base = zp(d)
        result = None
        for c in range(2):
            weight = w_all[pl.ds(base * span + c * (span // 2), span // 2)].reshape(span // 2 * wrows, -1)
            term = jnp.dot(a_all[base * 2 + c, rows, :], weight, preferred_element_type=F32)
            result = term if result is None else result + term
        return result

    def z_event(i, way):
        z_wait(i, way)
        if i + 4 < 4 * rz - 2:
            z_send(i + 4, way)
        d, part = z_item(i, way)
        hand(d - way, part)

    def run(events):
        for event in events:
            if event[0] == "z":
                z_event(*event[1:])
            else:
                w_event(event)

    run(AFTER_MIXED)
    halves = [pl.ds(part * half, half) for part in range(2)]
    for d in (0, -1, 1, -2, 2):
        for part in range(2):
            if d:
                acc[halves[part], :] += multiply(d, part)
            else:
                acc[halves[part], :] = multiply(d, part)
    run(AFTER_WEIGHTS)
    for d in (-3, 3):
        for part in range(2):
            acc[halves[part], :] += multiply(d, part)
    loads[4].wait()
    for part, d in ((0, -rz), (1, rz)):
        total = acc[halves[part], :] + multiply(d, part)
        out_ref[0, halves[part], :] = (res[halves[part], :].astype(F32) + total).astype(BF16)
    net.drain()


def local(dims, queries, keys, spike_counts, spike_scale, log_decay, norm_gain, out_weight, residual_in):
    ny, nz, heads, hs, block, wrows, xr = dims
    width = heads * hs
    columns = out_weight.shape[1]
    depth = heads * hs // NX + 16
    vmem = pl.BlockSpec(memory_space=pltpu.VMEM)
    hbm = pl.BlockSpec(memory_space=pltpu.HBM)
    return pl.pallas_call(
        functools.partial(kernel, dims),
        out_shape=pltpu.VMEM((1, block, columns), BF16),
        in_specs=[hbm] * 8,
        out_specs=vmem,
        scratch_shapes=[
            pltpu.VMEM((block, width), BF16),
            pltpu.VMEM((block, width), BF16),
            pltpu.VMEM((block, width), jnp.int32),
            pltpu.VMEM((1, width), F32),
            pltpu.VMEM((1, heads, block), F32),
            pltpu.VMEM((1, width), F32),
            pltpu.VMEM((block, columns), BF16),
            pltpu.VMEM((block, width), BF16),
            pltpu.VMEM((block, columns), F32),
            pltpu.VMEM((heads, block, hs), F32),
            pltpu.VMEM((heads, block, hs), F32),
            pltpu.VMEM((2 * nz, block, width), BF16),
            pltpu.VMEM((ny * NX, wrows, columns), BF16),
            pltpu.VMEM((NX, depth, hs), BF16),
            pltpu.VMEM((NX, depth, hs), BF16),
            pltpu.VMEM((depth, hs), BF16),
            pltpu.VMEM((ny - 1, depth, hs), BF16),
            pltpu.VMEM((NX, depth - 16, hs), BF16),
            pltpu.VMEM((NX, depth - 16, hs), BF16),
            pltpu.SemaphoreType.DMA((120,)),
            pltpu.SemaphoreType.DMA((120,)),
            pltpu.SemaphoreType.DMA((8,)),
        ],
        compiler_params=pltpu.CompilerParams(
            collective_id=0, has_side_effects=True, vmem_limit_bytes=60 * 1024 * 1024
        ),
    )(
        queries, keys, spike_counts, spike_scale.reshape(1, width), log_decay,
        norm_gain.reshape(1, width), out_weight, residual_in,
    )


def solution(mesh):
    ny, nz = mesh.shape["context"] // NX, mesh.shape["tensor"] // 2

    def whole(queries, keys, spike_counts, spike_scale, log_decay, norm_gain, out_weight, residual_in):
        heads = log_decay.shape[1] // (2 * nz)
        hs = queries.shape[2] // log_decay.shape[1]
        block = queries.shape[1] // (ny * NX)
        wrows = out_weight.shape[0] // (ny * NX)
        xr = wrows * 3 // 8
        dims = (ny, nz, heads, hs, block, wrows, xr)
        in_specs = (
            P(None, "context", "tensor"),
            P(None, "context", "tensor"),
            P(None, "context", "tensor"),
            P("tensor"),
            P(None, "tensor", "context"),
            P("tensor"),
            P("context", "tensor"),
            P(None, "context", "tensor"),
        )
        return jax.shard_map(
            functools.partial(local, dims),
            mesh=mesh,
            in_specs=in_specs,
            out_specs=P(None, "context", "tensor"),
            check_vma=False,
        )(queries, keys, spike_counts, spike_scale, log_decay, norm_gain, out_weight, residual_in)

    return whole
```
